32 devices in a mesh: group: 4 (over z), member: 8 (over y, x, core).
Axes of the slice: x: 2, y: 2, z: 4, core: 2. Of those that a mesh axis runs over, the one named last changes fastest.
Arguments:
- source: bfloat16 [32768, 256], P(('group', 'member')), may hold values from -6 to 6
- target: bfloat16 [8192, 256], P(('group', 'member')), may hold values from -6 to 6
- pair_source: int32 [32, 32], P(('group', 'member')), may hold values from 0 to 3, as said below
- pair_target: int32 [32, 32], P(('group', 'member')), may hold values from 0 to 15, as said below
- pair_count: int32 [32], P(('group', 'member')), may hold values from 4 to 32, as said below
Outputs:
- log_source: float32 [32768], P(('group', 'member'))
- log_target: float32 [8192], P(('group', 'member'))
The draws below stay inside these ranges and needn't reach their ends.
Inputs may be any that keep to these rules, and one draw needn't show every extreme that they name: `pair_source`: each entry is the device's own source tile, 0 to 3; slots 0 to 3 name each of them once, and no (source tile, window tile) pair stands twice on one device. `pair_target`: window index of the pair's target tile; on every device slot 0 names the device's own target tile (index equal to its member index). `pair_count`: at least 4; in every group one device has exactly 32.
All inputs are finite; a program needn't handle non-finite values.
Results may differ from the reference program's by a relative error of at most 0.0031.
Values may be sent and summed in bfloat16 or wider, within the bound.
No kernel may reach another device: no remote copies, remote signals or barrier semaphores. Data moves between devices by JAX's collectives and lax.ppermute only.
A program may use at most 128 MiB of HBM per device.

```python
import jax
import jax.numpy as jnp
from jax import lax

DL = 256
PATCH_SAMPLE_SIZE = 256
ST_DEV = 4
ITERS = 2
P_DEV = 32
NS = 32768
NT = 8192
N_GROUP = 4
N_MEMBER = 8
DEVICES = 32


def pair_table(key):
    base_key = jax.random.fold_in(key, 17)

    def one_device(device):
        device_key = jax.random.fold_in(base_key, device)
        orders = jax.vmap(lambda subkey: jax.random.permutation(subkey, 2 * N_MEMBER))(jax.random.split(device_key, ST_DEV))
        member = (device % N_MEMBER).astype(jnp.int32)
        first_order = orders[0].astype(jnp.int32)
        position = jnp.argmax(first_order == member).astype(jnp.int32)
        leading = first_order[0]
        first_order = first_order.at[position].set(leading).at[0].set(member)
        orders = orders.astype(jnp.int32).at[0].set(first_order)
        relabel = jax.random.permutation(jax.random.fold_in(device_key, 5), ST_DEV).astype(jnp.int32)
        targets = orders[:, :N_MEMBER].T.reshape(P_DEV)
        sources = jnp.tile(relabel, N_MEMBER)
        return (sources.astype(jnp.int32), targets.astype(jnp.int32))
    return jax.vmap(one_device)(jnp.arange(DEVICES, dtype=jnp.int32))


def draw_pair_source(key, part):
    return pair_table(key)[0]


def draw_pair_target(key, part):
    return pair_table(key)[1]


def draw_pair_count(key, part):
    count_key = jax.random.fold_in(key, 31)
    counts = jax.random.randint(jax.random.fold_in(count_key, 1), (DEVICES,), ST_DEV, P_DEV // 2 + 1).astype(jnp.int32)
    busiest = jax.random.randint(jax.random.fold_in(count_key, 2), (DEVICES // N_MEMBER,), 0, N_MEMBER).astype(jnp.int32)
    is_busiest = (jnp.arange(N_MEMBER, dtype=jnp.int32)[None, :] == busiest[:, None]).reshape(DEVICES)
    return jnp.where(is_busiest, P_DEV, counts).astype(jnp.int32)


def block_scale(key, dims, shards, least, top_value):
    def one(axis_at, shards_of):
        draws = jax.random.uniform(jax.random.fold_in(jax.random.fold_in(key, 6), axis_at), (shards_of,), jnp.float32, least / len(shards), top_value / len(shards))
        return jnp.repeat(jnp.exp(draws), dims[axis_at] // shards_of).reshape((-1,) + (1,) * (len(dims) - axis_at - 1))

    loudness = one(*shards[0])
    for cut in shards[1:]:
        loudness = loudness * one(*cut)
    return loudness


def normal_values(rng, extent, spread, most, shards=(), kind=jnp.bfloat16):
    entries = jax.random.normal(rng, extent, jnp.float32) * spread
    if len(shards) > 0:
        entries = block_scale(rng, extent, shards, -0.22, 0.18) * entries
    return jnp.clip(entries, min=-most, max=most).astype(kind)


def setup_inputs(seed: int = 0) -> dict:
    keys = jax.random.split(jax.random.key(seed), 6)
    source = normal_values(keys[0], (NS, DL), 1.0, 6.0, ((0, 32),))
    target = normal_values(keys[1], (NT, DL), 1.0, 6.0, ((0, 32),))
    pair_source = draw_pair_source(jax.random.fold_in(keys[5], 71), 0)
    pair_target = draw_pair_target(jax.random.fold_in(keys[5], 71), 0)
    pair_count = draw_pair_count(jax.random.fold_in(keys[5], 71), 0)
    return dict(source=source, target=target, pair_source=pair_source, pair_target=pair_target, pair_count=pair_count)


regularizer_strength = 0.05

def normalize(values):
    floats = values.astype(jnp.float32)
    return (floats / jnp.sqrt(lax.optimization_barrier(jnp.sum(floats * floats, axis=1, keepdims=True)) + 1e-06)).astype(jnp.bfloat16)

def reference(source, target, pair_source, pair_target, pair_count):
    unit_source = normalize(source).reshape(DEVICES, ST_DEV, PATCH_SAMPLE_SIZE, DL)
    unit_target = normalize(target).reshape(DEVICES, PATCH_SAMPLE_SIZE, DL)
    device_ids = jnp.arange(DEVICES, dtype=jnp.int32)
    home_group = device_ids // N_MEMBER
    target_tiles = ((home_group[:, None] + pair_target // N_MEMBER) % N_GROUP * N_MEMBER + pair_target % N_MEMBER).astype(jnp.int32)
    valid_mask = (jnp.arange(P_DEV, dtype=jnp.int32)[None, :] < pair_count[:, None]).astype(jnp.float32)
    scale_target = jnp.ones((DEVICES, PATCH_SAMPLE_SIZE), jnp.float32)
    scale_source = jnp.ones((DEVICES, ST_DEV, PATCH_SAMPLE_SIZE), jnp.float32)
    for sweep_number in range(ITERS):

        def per_device(device_items, scale_target=scale_target):
            sources, source_slots, tile_ids, surviving_indicator = device_items
            partners = unit_target[tile_ids].astype(jnp.float32)
            own_rows = sources[source_slots].astype(jnp.float32)
            similarity_logits = jnp.einsum('pid,pjd->pij', own_rows, partners, precision=lax.Precision.HIGHEST)
            boltzmann_factor_patches = jnp.exp(similarity_logits / regularizer_strength) / PATCH_SAMPLE_SIZE * surviving_indicator[:, None, None]
            boltzmann_factor_patches = lax.optimization_barrier(boltzmann_factor_patches.astype(jnp.bfloat16)).astype(jnp.float32)
            row_parts = jnp.einsum('pij,pj->pi', boltzmann_factor_patches, scale_target[tile_ids], precision=lax.Precision.HIGHEST)
            pick_source = (source_slots[:, None] == jnp.arange(ST_DEV, dtype=jnp.int32)[None, :]).astype(jnp.float32)
            row_sums = jnp.einsum('ps,pi->si', pick_source, row_parts, precision=lax.Precision.HIGHEST)
            source_scale = 1.0 / row_sums
            column_parts = jnp.einsum('pij,pi->pj', boltzmann_factor_patches, source_scale[source_slots], precision=lax.Precision.HIGHEST)
            return (source_scale, column_parts)
        scale_source, column_parts = lax.map(per_device, (unit_source, pair_source, target_tiles, valid_mask))
        columns = jax.ops.segment_sum(column_parts.reshape(DEVICES * P_DEV, PATCH_SAMPLE_SIZE), target_tiles.reshape(DEVICES * P_DEV), num_segments=DEVICES)
        scale_target = ST_DEV / columns
    return (jnp.log(scale_source).reshape(NS), jnp.log(scale_target).reshape(NT))
```

```python
import functools
import math

import jax
import jax.numpy as jnp
from jax import lax
from jax.experimental import pallas as pl
from jax.experimental.pallas import tpu as pltpu
from jax.sharding import PartitionSpec as P

ITERS = 2
REGULARIZER = 0.05
EPSILON = 1e-06
CORES = 2
LANES = 128


BOTH = ("group", "member")
VM = pl.BlockSpec(memory_space=pltpu.VMEM)
SM = pl.BlockSpec(memory_space=pltpu.SMEM)


def unit(values):
    floats = values.astype(jnp.float32)
    return (floats / jnp.sqrt(jnp.sum(floats * floats, axis=1, keepdims=True) + EPSILON)).astype(
        jnp.bfloat16
    )


def swap_member(x, bit):
    size = lax.axis_size("member")
    return lax.ppermute(x, "member", [(i, i ^ bit) for i in range(size)])


def shift_group(x, by):
    size = lax.axis_size("group")
    return lax.ppermute(x, "group", [(i, (i + by) % size) for i in range(size)])


def from_next_group(x, bit):
    groups, members = lax.axis_size("group"), lax.axis_size("member")
    return lax.ppermute(
        x,
        BOTH,
        [
            (g * members + m, (g - 1) % groups * members + (m ^ bit))
            for g in range(groups)
            for m in range(members)
        ],
    )


def rows_out(acc, out):
    tiles, cells, lanes = acc.shape
    lane = lax.broadcasted_iota(jnp.int32, (cells, lanes), 1)
    table = jnp.zeros((cells, lanes), jnp.float32)
    for s in range(tiles):
        table = jnp.where(lane == s, jnp.sum(acc[s], axis=1, keepdims=True), table)
    out[...] = jnp.transpose(table)[:tiles]


def build_kernel(chips, slots, *refs):
    targets = refs[: 2 * chips]
    own, other, mine, theirs = refs[2 * chips : 2 * chips + 4]
    factors, table, rows = refs[2 * chips + 4 : 2 * chips + 7]
    units, window, acc = refs[2 * chips + 7 :]
    cells = targets[0].shape[0]
    tiles = own.shape[0] // cells
    member = lax.axis_index("member")
    chip, core = member // CORES, lax.rem(member, CORES)
    for k in range(chips):
        at = jnp.bitwise_xor(chip, k)
        window[at] = unit(targets[k][...])
        window[chips + at] = unit(targets[chips + k][...])
    for half, raw in enumerate((own, other)):
        for s in range(tiles):
            units[half * tiles + s] = unit(raw[s * cells : (s + 1) * cells])
    acc[...] = jnp.zeros_like(acc)
    factor = 1.0 / REGULARIZER * math.log2(math.e)
    found = jnp.int32(0)
    for half, info in enumerate((mine, theirs)):

        def slot(k, found, half=half, info=info):
            label = info[0, slots + k]
            here = lax.rem(label, CORES) == core

            @pl.when(here)
            def _():
                s = half * tiles + info[0, k]
                w = label // CORES
                logits = lax.dot_general(
                    units[s],
                    window[w],
                    (((1,), (1,)), ((), ())),
                    preferred_element_type=jnp.float32,
                )
                values = jnp.exp2(logits * factor)
                factors[found] = values.astype(jnp.bfloat16)
                total = values[:, :LANES]
                for j in range(1, cells // LANES):
                    total = total + values[:, j * LANES : (j + 1) * LANES]
                acc[s] += total
                table[1 + 2 * found] = s
                table[2 + 2 * found] = w

            return found + here.astype(jnp.int32)

        found = lax.fori_loop(0, info[0, 2 * slots], slot, found)
    table[0] = found
    rows_out(acc, rows)


def row_kernel(factors, table, columns, before, after, rows, scale, acc):
    chips = before.shape[0]
    tiles = acc.shape[0] // CORES
    scale[:chips] = float(tiles) / (columns[:chips] + before[...])
    scale[chips:] = float(tiles) / (columns[chips:] + after[...])
    acc[...] = jnp.zeros_like(acc)
    cells = factors.shape[1]

    def pair(n, carry):
        s, w = table[1 + 2 * n], table[2 + 2 * n]
        values = factors[n].astype(jnp.float32) * scale[pl.ds(w, 1), :]
        total = values[:, :LANES]
        for j in range(1, cells // LANES):
            total = total + values[:, j * LANES : (j + 1) * LANES]
        acc[s] += total
        return carry

    lax.fori_loop(0, table[0], pair, 0)
    rows_out(acc, rows)


def column_kernel(last, factors, table, rows, arrived, columns, *rest):
    if last:
        logs, spread, acc = rest
    else:
        spread, acc = rest
    tiles = rows.shape[0] // CORES
    cells = factors.shape[1]
    total = rows[...] + jnp.concatenate([arrived[tiles:], arrived[:tiles]], 0)
    scale = 1.0 / total
    if last:
        logs[...] = jnp.log(scale[:tiles] * float(cells))
    flipped = jnp.transpose(scale)
    for s in range(CORES * tiles):
        spread[s] = jnp.broadcast_to(flipped[:, s : s + 1], (cells, LANES))
    acc[...] = jnp.zeros_like(acc)

    def pair(n, carry):
        s, w = table[1 + 2 * n], table[2 + 2 * n]
        values = factors[n].astype(jnp.float32)
        for j in range(cells // LANES):
            part = values[:, j * LANES : (j + 1) * LANES] * spread[s]
            acc[w, :, j * LANES : (j + 1) * LANES] += jnp.sum(
                part.reshape(cells // 8, 8, LANES), axis=0
            )
        return carry

    lax.fori_loop(0, table[0], pair, 0)
    columns[...] = jnp.sum(acc[...], axis=1)


def shards(source, target, pair_source, pair_target, pair_count):
    members = lax.axis_size("member")
    chips = members // CORES
    cells, width = target.shape
    tiles = source.shape[0] // cells
    slots = pair_source.shape[1]
    most = CORES * tiles * 2 * chips
    pair_most = min(CORES * slots, most)
    info = jnp.concatenate([pair_source, pair_target, pair_count[:, None]], 1)
    partner_info = swap_member(info, 1)
    partner_source = swap_member(source, 1)
    own_window = [target] + [swap_member(target, CORES * k) for k in range(1, chips)]
    next_window = [from_next_group(target, CORES * k) for k in range(chips)]

    limit = pltpu.CompilerParams(vmem_limit_bytes=60 * 2**20)
    f32 = jnp.float32
    vectors = jax.ShapeDtypeStruct((CORES * tiles, cells), f32)
    sums = jax.ShapeDtypeStruct((2 * chips, cells), f32)
    lanes_acc = pltpu.VMEM((CORES * tiles, cells, LANES), f32)
    factors, table, rows = pl.pallas_call(
        functools.partial(build_kernel, chips, slots),
        out_shape=(
            jax.ShapeDtypeStruct((pair_most, cells, cells), jnp.bfloat16),
            jax.ShapeDtypeStruct((1 + 2 * pair_most,), jnp.int32),
            vectors,
        ),
        in_specs=[VM] * (2 * chips + 2) + [SM] * 2,
        out_specs=(VM, SM, VM),
        scratch_shapes=[
            pltpu.VMEM((CORES * tiles, cells, width), jnp.bfloat16),
            pltpu.VMEM((2 * chips, cells, width), jnp.bfloat16),
            lanes_acc,
        ],
        compiler_params=limit,
        name="build",
    )(*own_window, *next_window, source, partner_source, info, partner_info)

    log_source = None
    own = None
    for sweep in range(ITERS):
        last = sweep + 1 == ITERS
        if sweep > 0:
            rows = pl.pallas_call(
                row_kernel,
                out_shape=vectors,
                in_specs=[VM, SM, VM, VM, VM],
                out_specs=VM,
                scratch_shapes=[pltpu.VMEM((2 * chips, cells), f32), lanes_acc],
                compiler_params=limit,
                name="rows",
            )(factors, table, columns, before, after)
        arrived = swap_member(rows, 1)
        found = pl.pallas_call(
            functools.partial(column_kernel, last),
            out_shape=(sums,) + ((jax.ShapeDtypeStruct((tiles, cells), f32),) if last else ()),
            in_specs=[VM, SM, VM, VM],
            out_specs=(VM,) + ((VM,) if last else ()),
            scratch_shapes=[lanes_acc, pltpu.VMEM((2 * chips, 8, cells), f32)],
            compiler_params=limit,
            name="columns",
        )(factors, table, rows, arrived)
        columns = found[0]
        bit = CORES
        while bit < members:
            columns = columns + swap_member(columns, bit)
            bit *= 2
        if not last:
            before = shift_group(columns[chips:], 1)
            after = shift_group(columns[:chips], -1)
        else:
            log_source = found[1]
            chip = lax.axis_index("member") // CORES
            given = lax.dynamic_slice_in_dim(columns, chips + chip, 1, 0)
            own = lax.dynamic_slice_in_dim(columns, chip, 1, 0) + shift_group(given, 1)
    return (
        log_source.reshape(tiles * cells),
        jnp.log(float(tiles) / own).reshape(cells),
    )


def solution(mesh):
    placed = (
        P(BOTH, None),
        P(BOTH, None),
        P(BOTH, None),
        P(BOTH, None),
        P(BOTH),
    )
    return jax.shard_map(
        shards,
        mesh=mesh,
        in_specs=placed,
        out_specs=(P(BOTH), P(BOTH)),
        check_vma=False,
    )
```

```python
import functools
import math

import jax
import jax.numpy as jnp
from jax import lax
from jax.experimental import pallas as pl
from jax.experimental.pallas import tpu as pltpu
from jax.sharding import PartitionSpec as P

ITERS = 2
REGULARIZER = 0.05
EPSILON = 1e-06
CORES = 2
LANES = 128


BOTH = ("group", "member")
VM = pl.BlockSpec(memory_space=pltpu.VMEM)
SM = pl.BlockSpec(memory_space=pltpu.SMEM)


def unit(values):
    floats = values.astype(jnp.float32)
    return (floats / jnp.sqrt(jnp.sum(floats * floats, axis=1, keepdims=True) + EPSILON)).astype(
        jnp.bfloat16
    )


def swap_member(x, bit):
    size = lax.axis_size("member")
    return lax.ppermute(x, "member", [(i, i ^ bit) for i in range(size)])


def shift_group(x, by):
    size = lax.axis_size("group")
    return lax.ppermute(x, "group", [(i, (i + by) % size) for i in range(size)])


def from_next_group(x, bit):
    groups, members = lax.axis_size("group"), lax.axis_size("member")
    return lax.ppermute(
        x,
        BOTH,
        [
            (g * members + m, (g - 1) % groups * members + (m ^ bit))
            for g in range(groups)
            for m in range(members)
        ],
    )


def rows_out(acc, out):
    tiles, cells, lanes = acc.shape
    lane = lax.broadcasted_iota(jnp.int32, (cells, lanes), 1)
    table = jnp.zeros((cells, lanes), jnp.float32)
    for s in range(tiles):
        table = jnp.where(lane == s, jnp.sum(acc[s], axis=1, keepdims=True), table)
    out[...] = jnp.transpose(table)[:tiles]


def build_kernel(chips, slots, *refs):
    targets = refs[: 2 * chips]
    own, other, mine, theirs = refs[2 * chips : 2 * chips + 4]
    factors, table, rows = refs[2 * chips + 4 : 2 * chips + 7]
    units, window, acc = refs[2 * chips + 7 :]
    cells = targets[0].shape[0]
    tiles = own.shape[0] // cells
    member = lax.axis_index("member")
    chip, core = member // CORES, lax.rem(member, CORES)
    for k in range(chips):
        at = jnp.bitwise_xor(chip, k)
        window[at] = unit(targets[k][...])
        window[chips + at] = unit(targets[chips + k][...])
    for half, raw in enumerate((own, other)):
        for s in range(tiles):
            units[half * tiles + s] = unit(raw[s * cells : (s + 1) * cells])
    acc[...] = jnp.zeros_like(acc)
    factor = 1.0 / REGULARIZER * math.log2(math.e)
    found = jnp.int32(0)
    for half, info in enumerate((mine, theirs)):

        def slot(k, found, half=half, info=info):
            label = info[0, slots + k]
            here = lax.rem(label, CORES) == core

            @pl.when(here)
            def _():
                s = half * tiles + info[0, k]
                w = label // CORES
                logits = lax.dot_general(
                    units[s],
                    window[w],
                    (((1,), (1,)), ((), ())),
                    preferred_element_type=jnp.float32,
                )
                values = jnp.exp2(logits * factor)
                factors[found] = values.astype(jnp.bfloat16)
                total = values[:, :LANES]
                for j in range(1, cells // LANES):
                    total = total + values[:, j * LANES : (j + 1) * LANES]
                acc[s] += total
                table[1 + 2 * found] = s
                table[2 + 2 * found] = w

            return found + here.astype(jnp.int32)

        found = lax.fori_loop(0, info[0, 2 * slots], slot, found)
    table[0] = found
    rows_out(acc, rows)


def row_kernel(factors, table, columns, before, after, rows, scale, acc):
    chips = before.shape[0]
    tiles = acc.shape[0] // CORES
    scale[:chips] = float(tiles) / (columns[:chips] + before[...])
    scale[chips:] = float(tiles) / (columns[chips:] + after[...])
    acc[...] = jnp.zeros_like(acc)
    cells = factors.shape[1]

    def pair(n, carry):
        s, w = table[1 + 2 * n], table[2 + 2 * n]
        values = factors[n].astype(jnp.float32) * scale[pl.ds(w, 1), :]
        total = values[:, :LANES]
        for j in range(1, cells // LANES):
            total = total + values[:, j * LANES : (j + 1) * LANES]
        acc[s] += total
        return carry

    lax.fori_loop(0, table[0], pair, 0)
    rows_out(acc, rows)


def column_kernel(last, factors, table, rows, arrived, columns, *rest):
    if last:
        logs, spread, acc = rest
    else:
        spread, acc = rest
    tiles = rows.shape[0] // CORES
    cells = factors.shape[1]
    total = rows[...] + jnp.concatenate([arrived[tiles:], arrived[:tiles]], 0)
    scale = 1.0 / total
    if last:
        logs[...] = jnp.log(scale[:tiles] * float(cells))
    flipped = jnp.transpose(scale)
    for s in range(CORES * tiles):
        spread[s] = jnp.broadcast_to(flipped[:, s : s + 1], (cells, LANES))
    acc[...] = jnp.zeros_like(acc)

    def pair(n, carry):
        s, w = table[1 + 2 * n], table[2 + 2 * n]
        values = factors[n].astype(jnp.float32)
        for j in range(cells // LANES):
            part = values[:, j * LANES : (j + 1) * LANES] * spread[s]
            acc[w, :, j * LANES : (j + 1) * LANES] += jnp.sum(
                part.reshape(cells // 8, 8, LANES), axis=0
            )
        return carry

    lax.fori_loop(0, table[0], pair, 0)
    columns[...] = jnp.sum(acc[...], axis=1)


def shards(source, target, pair_source, pair_target, pair_count):
    members = lax.axis_size("member")
    chips = members // CORES
    cells, width = target.shape
    tiles = source.shape[0] // cells
    slots = pair_source.shape[1]
    most = CORES * tiles * 2 * chips
    pair_most = min(CORES * slots, most)
    info = jnp.concatenate([pair_source, pair_target, pair_count[:, None]], 1)
    partner_info = swap_member(info, 1)
    partner_source = swap_member(source, 1)
    own_window = [target] + [swap_member(target, CORES * k) for k in range(1, chips)]
    next_window = [from_next_group(target, CORES * k) for k in range(chips)]

    held = pair_most * cells * cells * 2
    build_limit = pltpu.CompilerParams(vmem_limit_bytes=held + 10 * 2**20)
    limit = pltpu.CompilerParams(vmem_limit_bytes=held + 4 * 2**20)
    f32 = jnp.float32
    vectors = jax.ShapeDtypeStruct((CORES * tiles, cells), f32)
    sums = jax.ShapeDtypeStruct((2 * chips, cells), f32)
    lanes_acc = pltpu.VMEM((CORES * tiles, cells, LANES), f32)
    factors, table, rows = pl.pallas_call(
        functools.partial(build_kernel, chips, slots),
        out_shape=(
            jax.ShapeDtypeStruct((pair_most, cells, cells), jnp.bfloat16),
            jax.ShapeDtypeStruct((1 + 2 * pair_most,), jnp.int32),
            vectors,
        ),
        in_specs=[VM] * (2 * chips + 2) + [SM] * 2,
        out_specs=(VM, SM, VM),
        scratch_shapes=[
            pltpu.VMEM((CORES * tiles, cells, width), jnp.bfloat16),
            pltpu.VMEM((2 * chips, cells, width), jnp.bfloat16),
            lanes_acc,
        ],
        compiler_params=build_limit,
        name="build",
    )(*own_window, *next_window, source, partner_source, info, partner_info)

    log_source = None
    own = None
    for sweep in range(ITERS):
        last = sweep + 1 == ITERS
        if sweep > 0:
            rows = pl.pallas_call(
                row_kernel,
                out_shape=vectors,
                in_specs=[VM, SM, VM, VM, VM],
                out_specs=VM,
                scratch_shapes=[pltpu.VMEM((2 * chips, cells), f32), lanes_acc],
                compiler_params=limit,
                name="rows",
            )(factors, table, columns, before, after)
        arrived = swap_member(rows, 1)
        found = pl.pallas_call(
            functools.partial(column_kernel, last),
            out_shape=(sums,) + ((jax.ShapeDtypeStruct((tiles, cells), f32),) if last else ()),
            in_specs=[VM, SM, VM, VM],
            out_specs=(VM,) + ((VM,) if last else ()),
            scratch_shapes=[lanes_acc, pltpu.VMEM((2 * chips, 8, cells), f32)],
            compiler_params=limit,
            name="columns",
        )(factors, table, rows, arrived)
        columns = found[0]
        bit = CORES
        while bit < members:
            columns = columns + swap_member(columns, bit)
            bit *= 2
        if not last:
            before = shift_group(columns[chips:], 1)
            after = shift_group(columns[:chips], -1)
        else:
            log_source = found[1]
            chip = lax.axis_index("member") // CORES
            given = lax.dynamic_slice_in_dim(columns, chips + chip, 1, 0)
            own = lax.dynamic_slice_in_dim(columns, chip, 1, 0) + shift_group(given, 1)
    return (
        log_source.reshape(tiles * cells),
        jnp.log(float(tiles) / own).reshape(cells),
    )


def solution(mesh):
    placed = (
        P(BOTH, None),
        P(BOTH, None),
        P(BOTH, None),
        P(BOTH, None),
        P(BOTH),
    )
    return jax.shard_map(
        shards,
        mesh=mesh,
        in_specs=placed,
        out_specs=(P(BOTH), P(BOTH)),
        check_vma=False,
    )
```

```python
import functools
import math

import jax
import jax.numpy as jnp
from jax import lax
from jax.experimental import pallas as pl
from jax.experimental.pallas import tpu as pltpu
from jax.sharding import PartitionSpec as P

ITERS = 2
REGULARIZER = 0.05
EPSILON = 1e-06
CORES = 2
LANES = 128
MIB = 2**20


BOTH = ("group", "member")
VM = pl.BlockSpec(memory_space=pltpu.VMEM)
SM = pl.BlockSpec(memory_space=pltpu.SMEM)
ANY = pl.BlockSpec(memory_space=pl.ANY)
F32 = jnp.float32
BF16 = jnp.bfloat16
FACTOR = math.log2(math.e) / REGULARIZER


def odd(bits):
    return bin(bits).count("1") % 2


def odd_traced(value, width):
    result = jnp.int32(0)
    for b in range(width):
        result = result ^ (value >> b)
    return result & 1


def hop(x, up, bits):
    groups, members = lax.axis_size("group"), lax.axis_size("member")
    turn = odd(bits) ^ ((up & 1) if groups % 2 == 0 else 0)
    mask = CORES * bits + turn
    return lax.ppermute(
        x,
        BOTH,
        [
            (g * members + m, (g - up) % groups * members + (m ^ mask))
            for g in range(groups)
            for m in range(members)
        ],
    )


def partner(x):
    size = lax.axis_size("member")
    return lax.ppermute(x, "member", [(i, i ^ 1) for i in range(size)])


def spread_tiles(start, chips):
    half = start.shape[0] // 2
    tiles = {0: [start]}

    def part(k, which):
        blocks = tiles[k]
        return blocks[which] if len(blocks) == 2 else blocks[0][which * half : (which + 1) * half]

    for k in sorted(range(1, chips), key=lambda k: (bin(k).count("1"), k)):
        low, high = k & -k, 1 << (k.bit_length() - 1)
        if low == high:
            tiles[k] = [hop(start, 0, k)]
        else:
            tiles[k] = [hop(part(k ^ high, 0), 0, high), hop(part(k ^ low, 1), 0, low)]
    return [tiles[k] for k in range(chips)]


def unit(values):
    floats = values.astype(F32)
    return (floats / jnp.sqrt(jnp.sum(floats * floats, axis=1, keepdims=True) + EPSILON)).astype(
        BF16
    )


def rows_out(acc, out):
    tiles, cells, lanes = acc.shape
    lane = lax.broadcasted_iota(jnp.int32, (cells, lanes), 1)
    table = jnp.zeros((cells, lanes), F32)
    for s in range(tiles):
        table = jnp.where(lane == s, jnp.sum(acc[s], axis=1, keepdims=True), table)
    out[...] = jnp.transpose(table)[:tiles]


def add_halves(acc, s, values):
    total = values[:, :LANES]
    for j in range(1, values.shape[1] // LANES):
        total = total + values[:, j * LANES : (j + 1) * LANES]
    acc[s] += total


def prepare_kernel(
    chips, slots, even, own, target, other, mine, theirs, units, home, first, second, raw, tile, done
):
    cells = units.shape[1]
    tiles = own.shape[0] // cells
    fetch = pltpu.make_async_copy(own, raw, done.at[0])
    fetch_home = pltpu.make_async_copy(target, tile, done.at[1])
    fetch.start()
    fetch_home.start()
    members = CORES * chips
    width = members.bit_length()
    member = lax.axis_index("member")
    chip = member // CORES
    kind = odd_traced(member, width)
    counts = (jnp.int32(0), jnp.int32(0))
    for half, info in enumerate((mine, theirs)):

        def slot(k, counts, half=half, info=info):
            early, late = counts
            label = info[0, slots + k]
            w = label // CORES
            beyond = (label >= members).astype(jnp.int32)
            place = lax.rem(label, members)
            here = (odd_traced(place, width) ^ (beyond & even)) == kind
            is_late = jnp.logical_and(beyond == 1, place // CORES != chip)
            s = half * tiles + info[0, k]
            to_early = jnp.logical_and(here, jnp.logical_not(is_late))
            to_late = jnp.logical_and(here, is_late)

            @pl.when(to_early)
            def _():
                first[1 + 2 * early] = s
                first[2 + 2 * early] = w

            @pl.when(to_late)
            def _():
                second[1 + 2 * late] = s
                second[2 + 2 * late] = w

            return early + to_early.astype(jnp.int32), late + to_late.astype(jnp.int32)

        counts = lax.fori_loop(0, info[0, 2 * slots], slot, counts)
    first[0], second[0] = counts
    for s in range(tiles):
        units[tiles + s] = unit(other[s * cells : (s + 1) * cells])
    fetch.wait()
    for s in range(tiles):
        units[s] = unit(raw[s * cells : (s + 1) * cells])
    fetch_home.wait()
    home[...] = unit(tile[...])


def place(window, at, blocks):
    row = 0
    for block in blocks:
        rows = block.shape[0]
        window[at, row : row + rows] = unit(block[...])
        row += rows


def build_pairs(units, window, table, factors, acc, where):
    def pair(n, carry):
        s, w = table[1 + 2 * n], table[2 + 2 * n]
        logits = lax.dot_general(
            units[s], window[where(w)], (((1,), (1,)), ((), ())), preferred_element_type=F32
        )
        values = jnp.exp2(logits * FACTOR)
        factors[n] = values.astype(BF16)
        add_halves(acc, s, values)
        return carry

    lax.fori_loop(0, table[0], pair, 0)


def first_kernel(chips, shape, units, table, home, *refs):
    count = sum(shape)
    tiles = refs[:count]
    factors, acc, window = refs[count:]
    chip = lax.axis_index("member") // CORES
    window[chip] = home[...]
    at = 0
    for k, blocks in enumerate(shape):
        slot = chip ^ (k + 1) if k + 1 < chips else chips
        place(window, slot, tiles[at : at + blocks])
        at += blocks
    acc[...] = jnp.zeros_like(acc)
    build_pairs(units, window, table, factors, acc, lambda w: jnp.minimum(w, chips))


def second_kernel(chips, shape, units, table, before, *refs):
    count = sum(shape)
    tiles = refs[:count]
    factors, rows, acc, window = refs[count:]
    chip = lax.axis_index("member") // CORES
    at = 0
    for k, blocks in enumerate(shape):
        place(window, chip ^ (k + 1), tiles[at : at + blocks])
        at += blocks
    acc[...] = before[...]
    build_pairs(units, window, table, factors, acc, lambda w: w - chips)
    rows_out(acc, rows)


def row_kernel(first, second, lists_first, lists_second, columns, before, after, rows, scale, acc):
    chips = before.shape[0]
    tiles = acc.shape[0] // CORES
    scale[:chips] = float(tiles) / (columns[:chips] + before[...])
    scale[chips:] = float(tiles) / (columns[chips:] + after[...])
    acc[...] = jnp.zeros_like(acc)
    for factors, table in ((first, lists_first), (second, lists_second)):

        def pair(n, carry, factors=factors, table=table):
            s, w = table[1 + 2 * n], table[2 + 2 * n]
            add_halves(acc, s, factors[n].astype(F32) * scale[pl.ds(w, 1), :])
            return carry

        lax.fori_loop(0, table[0], pair, 0)
    rows_out(acc, rows)


def column_kernel(last, first, second, lists_first, lists_second, rows, arrived, columns, *rest):
    if last:
        logs, spread, acc = rest
    else:
        spread, acc = rest
    tiles = rows.shape[0] // CORES
    cells = first.shape[1]
    total = rows[...] + jnp.concatenate([arrived[tiles:], arrived[:tiles]], 0)
    scale = 1.0 / total
    if last:
        logs[...] = jnp.log(scale[:tiles] * float(cells))
    flipped = jnp.transpose(scale)
    for s in range(CORES * tiles):
        spread[s] = jnp.broadcast_to(flipped[:, s : s + 1], (cells, LANES))
    acc[...] = jnp.zeros_like(acc)
    for factors, table in ((first, lists_first), (second, lists_second)):

        def pair(n, carry, factors=factors, table=table):
            s, w = table[1 + 2 * n], table[2 + 2 * n]
            values = factors[n].astype(F32)
            for j in range(cells // LANES):
                part = values[:, j * LANES : (j + 1) * LANES] * spread[s]
                acc[w, :, j * LANES : (j + 1) * LANES] += jnp.sum(
                    part.reshape(cells // 8, 8, LANES), axis=0
                )
            return carry

        lax.fori_loop(0, table[0], pair, 0)
    columns[...] = jnp.sum(acc[...], axis=1)


def shards(source, target, pair_source, pair_target, pair_count):
    groups, members = lax.axis_size("group"), lax.axis_size("member")
    chips = members // CORES
    cells, width = target.shape
    tiles = source.shape[0] // cells
    both = CORES * tiles
    slots = pair_source.shape[1]
    even = 1 if groups % 2 == 0 else 0
    most_first = min(CORES * slots, both * (chips + 1))
    most_second = min(CORES * slots, both * (chips - 1))

    beyond = hop(target, 1, 0)
    own_tiles = spread_tiles(target, chips)
    next_tiles = spread_tiles(beyond, chips)
    info = jnp.concatenate([pair_source, pair_target, pair_count[:, None]], 1)
    partner_source = partner(source)
    partner_info = partner(info)

    def shaped(*dims, kind=F32):
        return jax.ShapeDtypeStruct(dims, kind)

    def limit(size):
        return pltpu.CompilerParams(vmem_limit_bytes=int(size))

    def cost(pairs):
        return pl.CostEstimate(
            flops=2 * pairs * cells * cells * width,
            transcendentals=pairs * cells * cells,
            bytes_accessed=pairs * cells * cells * 2,
        )

    tile = cells * width * 2
    lanes_acc = (both, cells, LANES)
    units, home, lists_first, lists_second = pl.pallas_call(
        functools.partial(prepare_kernel, chips, slots, even),
        out_shape=(
            shaped(both, cells, width, kind=BF16),
            shaped(cells, width, kind=BF16),
            shaped(1 + 2 * most_first, kind=jnp.int32),
            shaped(1 + 2 * most_second, kind=jnp.int32),
        ),
        in_specs=[ANY, ANY, VM, SM, SM],
        out_specs=(VM, VM, SM, SM),
        scratch_shapes=[
            pltpu.VMEM(source.shape, BF16),
            pltpu.VMEM(target.shape, BF16),
            pltpu.SemaphoreType.DMA((2,)),
        ],
        compiler_params=limit(4 * MIB),
        cost_estimate=cost(both),
        name="prepare",
    )(source, target, partner_source, info, partner_info)

    early = own_tiles[1:] + [next_tiles[0]]
    late = next_tiles[1:]
    first, acc = pl.pallas_call(
        functools.partial(first_kernel, chips, [len(t) for t in early]),
        out_shape=(shaped(most_first, cells, cells, kind=BF16), shaped(*lanes_acc)),
        in_specs=[VM, SM, VM] + [VM] * sum(len(t) for t in early),
        out_specs=(VM, VM),
        scratch_shapes=[pltpu.VMEM((chips + 1, cells, width), BF16)],
        compiler_params=limit((most_first + 2 * chips + 2 + both) * tile + 5 * MIB),
        cost_estimate=cost(most_first),
        name="first",
    )(units, lists_first, home, *[b for t in early for b in t])
    second, rows = pl.pallas_call(
        functools.partial(second_kernel, chips, [len(t) for t in late]),
        out_shape=(shaped(most_second, cells, cells, kind=BF16), shaped(both, cells)),
        in_specs=[VM, SM, VM] + [VM] * sum(len(t) for t in late),
        out_specs=(VM, VM),
        scratch_shapes=[pltpu.VMEM(lanes_acc, F32), pltpu.VMEM((chips, cells, width), BF16)],
        compiler_params=limit((most_second + 2 * chips + both) * tile + 5 * MIB),
        cost_estimate=cost(most_second),
        name="second",
    )(units, lists_second, acc, *[b for t in late for b in t])
    held = (first, second, lists_first, lists_second)
    held_limit = limit((most_first + most_second) * tile + 4 * MIB)

    for sweep in range(ITERS):
        last = sweep + 1 == ITERS
        if sweep > 0:
            rows = pl.pallas_call(
                row_kernel,
                out_shape=shaped(both, cells),
                in_specs=[VM, VM, SM, SM, VM, VM, VM],
                out_specs=VM,
                scratch_shapes=[pltpu.VMEM((2 * chips, cells), F32), pltpu.VMEM(lanes_acc, F32)],
                compiler_params=held_limit,
                name="rows",
            )(*held, columns, before, after)
        found = pl.pallas_call(
            functools.partial(column_kernel, last),
            out_shape=(shaped(2 * chips, cells),) + ((shaped(tiles, cells),) if last else ()),
            in_specs=[VM, VM, SM, SM, VM, VM],
            out_specs=(VM,) + ((VM,) if last else ()),
            scratch_shapes=[
                pltpu.VMEM(lanes_acc, F32),
                pltpu.VMEM((2 * chips, 8, cells), F32),
            ],
            compiler_params=held_limit,
            name="columns",
        )(*held, rows, partner(rows))
        columns = found[0]
        bits = [1 << b for b in range(chips.bit_length() - 1)]
        if not last:
            for bit in bits:
                columns = columns + hop(columns, 0, bit)
            before = hop(columns[chips:], -1, 0)
            after = hop(columns[:chips], 1, 0)
        else:
            chip = lax.axis_index("member") // CORES
            for bit in bits[:-1]:
                columns = columns + hop(columns, 0, bit)
            far = bits[-1]

            def row(index):
                return lax.dynamic_slice_in_dim(columns, index, 1, 0)

            own = row(chip)
            own = own + hop(row(chip ^ far), 0, far)
            own = own + hop(row(chips + chip), -1, 0)
            own = own + hop(row(chips + (chip ^ far)), -1, far)
    return (
        found[1].reshape(tiles * cells),
        jnp.log(float(tiles) / own).reshape(cells),
    )


def solution(mesh):
    placed = (
        P(BOTH, None),
        P(BOTH, None),
        P(BOTH, None),
        P(BOTH, None),
        P(BOTH),
    )
    return jax.shard_map(
        shards,
        mesh=mesh,
        in_specs=placed,
        out_specs=(P(BOTH), P(BOTH)),
        check_vma=False,
    )
```

```python
import functools
import math

import jax
import jax.numpy as jnp
from jax import lax
from jax.experimental import pallas as pl
from jax.experimental.pallas import tpu as pltpu
from jax.sharding import PartitionSpec as P


ITERS = 2
REGULARIZER = 0.05
EPSILON = 1e-06
CORES = 2
LANES = 128
MIB = 2**20


BOTH = ("group", "member")
VM = pl.BlockSpec(memory_space=pltpu.VMEM)
SM = pl.BlockSpec(memory_space=pltpu.SMEM)
HB = pl.BlockSpec(memory_space=pltpu.HBM)
F32 = jnp.float32
BF16 = jnp.bfloat16
FACTOR = math.log2(math.e) / REGULARIZER


def odd(bits):
    return bin(bits).count("1") % 2


def odd_traced(value, width):
    result = jnp.int32(0)
    for b in range(width):
        result = result ^ (value >> b)
    return result & 1


def hop(x, up, bits):
    groups, members = lax.axis_size("group"), lax.axis_size("member")
    turn = odd(bits) ^ ((up & 1) if groups % 2 == 0 else 0)
    mask = CORES * bits + turn
    return lax.ppermute(
        x,
        BOTH,
        [
            (g * members + m, (g - up) % groups * members + (m ^ mask))
            for g in range(groups)
            for m in range(members)
        ],
    )


def partner(x):
    size = lax.axis_size("member")
    return lax.ppermute(x, "member", [(i, i ^ 1) for i in range(size)])


def spread_tiles(start, chips):
    half = start.shape[0] // 2
    tiles = {0: [start]}

    def part(k, which):
        blocks = tiles[k]
        return blocks[which] if len(blocks) == 2 else blocks[0][which * half : (which + 1) * half]

    for k in sorted(range(1, chips), key=lambda k: (bin(k).count("1"), k)):
        low, high = k & -k, 1 << (k.bit_length() - 1)
        if low == high:
            tiles[k] = [hop(start, 0, k)]
        else:
            upper = hop(part(k ^ high, 0), 0, high)
            tiles[k] = [upper, hop(part(k ^ low, 1), 0, low)]
    return [tiles[k] for k in range(chips)]


def unit(values):
    floats = values.astype(F32)
    return (floats / jnp.sqrt(jnp.sum(floats * floats, axis=1, keepdims=True) + EPSILON)).astype(
        BF16
    )


def rows_out(acc, out):
    tiles, cells, lanes = acc.shape
    lane = lax.broadcasted_iota(jnp.int32, (cells, lanes), 1)
    table = jnp.zeros((cells, lanes), F32)
    for s in range(tiles):
        table = jnp.where(lane == s, jnp.sum(acc[s], axis=1, keepdims=True), table)
    out[...] = jnp.transpose(table)[:tiles]


def add_halves(acc, s, values):
    total = values[:, :LANES]
    for j in range(1, values.shape[1] // LANES):
        total = total + values[:, j * LANES : (j + 1) * LANES]
    acc[s] += total


def prepare_kernel(
    chips, slots, even, own, target, other, mine, theirs, units, home, first, second, raw, tile, done
):
    cells = units.shape[1]
    tiles = own.shape[0] // cells
    fetch = pltpu.make_async_copy(own, raw, done.at[0])
    fetch_home = pltpu.make_async_copy(target, tile, done.at[1])
    fetch.start()
    fetch_home.start()
    members = CORES * chips
    width = members.bit_length()
    member = lax.axis_index("member")
    chip = member // CORES
    kind = odd_traced(member, width)
    counts = (jnp.int32(0), jnp.int32(0))
    for half, info in enumerate((mine, theirs)):

        def slot(k, counts, half=half, info=info):
            early, late = counts
            label = info[0, slots + k]
            w = label // CORES
            beyond = (label >= members).astype(jnp.int32)
            place = lax.rem(label, members)
            here = (odd_traced(place, width) ^ (beyond & even)) == kind
            is_late = jnp.logical_and(beyond == 1, place // CORES != chip)
            s = half * tiles + info[0, k]
            to_early = jnp.logical_and(here, jnp.logical_not(is_late))
            to_late = jnp.logical_and(here, is_late)

            @pl.when(to_early)
            def _():
                first[1 + 2 * early] = s
                first[2 + 2 * early] = w

            @pl.when(to_late)
            def _():
                second[1 + 2 * late] = s
                second[2 + 2 * late] = w

            return early + to_early.astype(jnp.int32), late + to_late.astype(jnp.int32)

        counts = lax.fori_loop(0, info[0, 2 * slots], slot, counts)
    first[0], second[0] = counts
    for s in range(tiles):
        units[tiles + s] = unit(other[s * cells : (s + 1) * cells])
    fetch.wait()
    for s in range(tiles):
        units[s] = unit(raw[s * cells : (s + 1) * cells])
    fetch_home.wait()
    home[...] = unit(tile[...])


def place(window, at, blocks):
    row = 0
    for block in blocks:
        rows = block.shape[0]
        window[at, row : row + rows] = unit(block[...])
        row += rows


def build_pairs(units, window, table, factors, acc, where):
    def pair(n, carry):
        s, w = table[1 + 2 * n], table[2 + 2 * n]
        logits = lax.dot_general(
            units[s], window[where(w)], (((1,), (1,)), ((), ())), preferred_element_type=F32
        )
        values = jnp.exp2(logits * FACTOR)
        factors[n] = values.astype(BF16)
        add_halves(acc, s, values)
        return carry

    lax.fori_loop(0, table[0], pair, 0)


def first_kernel(chips, shape, units, table, home, *refs):
    count = sum(shape)
    tiles = refs[:count]
    factors, acc, window = refs[count:]
    chip = lax.axis_index("member") // CORES
    window[chip] = home[...]
    at = 0
    for k, blocks in enumerate(shape):
        slot = chip ^ (k + 1) if k + 1 < chips else chips
        place(window, slot, tiles[at : at + blocks])
        at += blocks
    acc[...] = jnp.zeros_like(acc)
    build_pairs(units, window, table, factors, acc, lambda w: jnp.minimum(w, chips))


def second_kernel(chips, shape, units, table, before, *refs):
    count = sum(shape)
    tiles = refs[:count]
    factors, rows, acc, window = refs[count:]
    chip = lax.axis_index("member") // CORES
    at = 0
    for k, blocks in enumerate(shape):
        place(window, chip ^ (k + 1), tiles[at : at + blocks])
        at += blocks
    acc[...] = before[...]
    build_pairs(units, window, table, factors, acc, lambda w: w - chips)
    rows_out(acc, rows)


def row_kernel(first, second, lists_first, lists_second, columns, before, after, rows, scale, acc):
    chips = before.shape[0]
    tiles = acc.shape[0] // CORES
    scale[:chips] = float(tiles) / (columns[:chips] + before[...])
    scale[chips:] = float(tiles) / (columns[chips:] + after[...])
    acc[...] = jnp.zeros_like(acc)
    for factors, table in ((first, lists_first), (second, lists_second)):

        def pair(n, carry, factors=factors, table=table):
            s, w = table[1 + 2 * n], table[2 + 2 * n]
            add_halves(acc, s, factors[n].astype(F32) * scale[pl.ds(w, 1), :])
            return carry

        lax.fori_loop(0, table[0], pair, 0)
    rows_out(acc, rows)


def column_kernel(last, first, second, lists_first, lists_second, rows, arrived, columns, *rest):
    if last:
        logs, spread, acc = rest
    else:
        spread, acc = rest
    tiles = rows.shape[0] // CORES
    cells = first.shape[1]
    total = rows[...] + jnp.concatenate([arrived[tiles:], arrived[:tiles]], 0)
    scale = 1.0 / total
    if last:
        logs[...] = jnp.log(scale[:tiles] * float(cells))
    flipped = jnp.transpose(scale)
    for s in range(CORES * tiles):
        spread[s] = jnp.broadcast_to(flipped[:, s : s + 1], (cells, LANES))
    acc[...] = jnp.zeros_like(acc)
    for factors, table in ((first, lists_first), (second, lists_second)):

        def pair(n, carry, factors=factors, table=table):
            s, w = table[1 + 2 * n], table[2 + 2 * n]
            values = factors[n].astype(F32)
            for j in range(cells // LANES):
                part = values[:, j * LANES : (j + 1) * LANES] * spread[s]
                acc[w, :, j * LANES : (j + 1) * LANES] += jnp.sum(
                    part.reshape(cells // 8, 8, LANES), axis=0
                )
            return carry

        lax.fori_loop(0, table[0], pair, 0)
    columns[...] = jnp.sum(acc[...], axis=1)


def step(source, target, pair_source, pair_target, pair_count):
    groups, members = lax.axis_size("group"), lax.axis_size("member")
    chips = members // CORES
    cells, width = target.shape
    tiles = source.shape[0] // cells
    both = CORES * tiles
    slots = pair_source.shape[1]
    even = 1 if groups % 2 == 0 else 0
    most_first = min(CORES * slots, both * (chips + 1))
    most_second = min(CORES * slots, both * (chips - 1))

    beyond = hop(target, 1, 0)
    own_tiles = spread_tiles(target, chips)
    next_tiles = spread_tiles(beyond, chips)
    info = jnp.concatenate([pair_source, pair_target, pair_count[:, None]], 1)
    partner_source = partner(source)
    partner_info = partner(info)

    def shaped(*dims, kind=F32):
        return jax.ShapeDtypeStruct(dims, kind)

    def limit(size):
        return pltpu.CompilerParams(vmem_limit_bytes=int(size))

    def cost(pairs):
        return pl.CostEstimate(
            flops=2 * pairs * cells * cells * width,
            transcendentals=pairs * cells * cells,
            bytes_accessed=pairs * cells * cells * 2,
        )

    tile = cells * width * 2
    lanes_acc = (both, cells, LANES)
    prepare = pl.pallas_call(
        functools.partial(prepare_kernel, chips, slots, even),
        out_shape=(
            shaped(both, cells, width, kind=BF16),
            shaped(cells, width, kind=BF16),
            shaped(1 + 2 * most_first, kind=jnp.int32),
            shaped(1 + 2 * most_second, kind=jnp.int32),
        ),
        in_specs=[HB, HB, VM, SM, SM],
        out_specs=(VM, VM, SM, SM),
        scratch_shapes=[
            pltpu.VMEM(source.shape, BF16),
            pltpu.VMEM(target.shape, BF16),
            pltpu.SemaphoreType.DMA((2,)),
        ],
        compiler_params=limit(4 * MIB),
        cost_estimate=cost(both),
        name="prepare",
    )
    units, home, lists_first, lists_second = prepare(
        source, target, partner_source, info, partner_info
    )

    early = own_tiles[1:] + [next_tiles[0]]
    late = next_tiles[1:]
    first_call = pl.pallas_call(
        functools.partial(first_kernel, chips, [len(t) for t in early]),
        out_shape=(shaped(most_first, cells, cells, kind=BF16), shaped(*lanes_acc)),
        in_specs=[VM, SM, VM] + [VM] * sum(len(t) for t in early),
        out_specs=(VM, VM),
        scratch_shapes=[pltpu.VMEM((chips + 1, cells, width), BF16)],
        compiler_params=limit((most_first + 2 * chips + 2 + both) * tile + 5 * MIB),
        cost_estimate=cost(most_first),
        name="first",
    )
    first, acc = first_call(units, lists_first, home, *[b for t in early for b in t])
    second, rows = pl.pallas_call(
        functools.partial(second_kernel, chips, [len(t) for t in late]),
        out_shape=(shaped(most_second, cells, cells, kind=BF16), shaped(both, cells)),
        in_specs=[VM, SM, VM] + [VM] * sum(len(t) for t in late),
        out_specs=(VM, VM),
        scratch_shapes=[pltpu.VMEM(lanes_acc, F32), pltpu.VMEM((chips, cells, width), BF16)],
        compiler_params=limit((most_second + 2 * chips + both) * tile + 5 * MIB),
        cost_estimate=cost(most_second),
        name="second",
    )(units, lists_second, acc, *[b for t in late for b in t])
    held = (first, second, lists_first, lists_second)
    held_limit = limit((most_first + most_second) * tile + 4 * MIB)

    for sweep in range(ITERS):
        last = sweep + 1 == ITERS
        if sweep > 0:
            rows = pl.pallas_call(
                row_kernel,
                out_shape=shaped(both, cells),
                in_specs=[VM, VM, SM, SM, VM, VM, VM],
                out_specs=VM,
                scratch_shapes=[pltpu.VMEM((2 * chips, cells), F32), pltpu.VMEM(lanes_acc, F32)],
                compiler_params=held_limit,
                name="rows",
            )(*held, columns, before, after)
        found = pl.pallas_call(
            functools.partial(column_kernel, last),
            out_shape=(shaped(2 * chips, cells),) + ((shaped(tiles, cells),) if last else ()),
            in_specs=[VM, VM, SM, SM, VM, VM],
            out_specs=(VM,) + ((VM,) if last else ()),
            scratch_shapes=[
                pltpu.VMEM(lanes_acc, F32),
                pltpu.VMEM((2 * chips, 8, cells), F32),
            ],
            compiler_params=held_limit,
            name="columns",
        )(*held, rows, partner(rows))
        columns = found[0]
        bits = [1 << b for b in range(chips.bit_length() - 1)]
        if not last:
            for bit in bits:
                columns = columns + hop(columns, 0, bit)
            before = hop(columns[chips:], -1, 0)
            after = hop(columns[:chips], 1, 0)
        else:
            chip = lax.axis_index("member") // CORES
            for bit in bits[:-1]:
                columns = columns + hop(columns, 0, bit)
            far = bits[-1]

            def row(index):
                return lax.dynamic_slice_in_dim(columns, index, 1, 0)

            own = row(chip)
            own = own + hop(row(chip ^ far), 0, far)
            own = own + hop(row(chips + chip), -1, 0)
            own = own + hop(row(chips + (chip ^ far)), -1, far)
    return (
        found[1].reshape(tiles * cells),
        jnp.log(float(tiles) / own).reshape(cells),
    )


def solution(mesh):
    placed = (
        P(BOTH, None),
        P(BOTH, None),
        P(BOTH, None),
        P(BOTH, None),
        P(BOTH),
    )
    return jax.shard_map(
        step,
        mesh=mesh,
        in_specs=placed,
        out_specs=(P(BOTH), P(BOTH)),
        check_vma=False,
    )
```

```python
import functools
import math

import jax
import jax.numpy as jnp
from jax import lax
from jax.experimental import pallas as pl
from jax.experimental.pallas import tpu as pltpu
from jax.sharding import PartitionSpec as P


ITERS = 2
REGULARIZER = 0.05
EPSILON = 1e-06
CORES = 2
LANES = 128
MIB = 2**20
GROUP = 4


BOTH = ("group", "member")
VM = pl.BlockSpec(memory_space=pltpu.VMEM)
SM = pl.BlockSpec(memory_space=pltpu.SMEM)
HB = pl.BlockSpec(memory_space=pltpu.HBM)
F32 = jnp.float32
BF16 = jnp.bfloat16
FACTOR = math.log2(math.e) / REGULARIZER


def odd(bits):
    return bin(bits).count("1") % 2


def odd_traced(value, width):
    result = jnp.int32(0)
    for b in range(width):
        result = result ^ (value >> b)
    return result & 1


def up_to_group(count):
    return -(-count // GROUP) * GROUP


def hop(x, up, bits):
    groups, members = lax.axis_size("group"), lax.axis_size("member")
    turn = odd(bits) ^ ((up & 1) if groups % 2 == 0 else 0)
    mask = CORES * bits + turn
    return lax.ppermute(
        x,
        BOTH,
        [
            (g * members + m, (g - up) % groups * members + (m ^ mask))
            for g in range(groups)
            for m in range(members)
        ],
    )


def partner(x):
    size = lax.axis_size("member")
    return lax.ppermute(x, "member", [(i, i ^ 1) for i in range(size)])


def spread_tiles(start, chips):
    tiles = [start]
    for k in range(1, chips):
        tiles.append(hop(start, 0, k))
    return tiles


def unit(values):
    floats = values.astype(F32)
    return (floats / jnp.sqrt(jnp.sum(floats * floats, axis=1, keepdims=True) + EPSILON)).astype(
        BF16
    )


def rows_out(acc, out):
    tiles = out.shape[0]
    cells, lanes = acc.shape[1:]
    lane = lax.broadcasted_iota(jnp.int32, (cells, lanes), 1)
    table = jnp.zeros((cells, lanes), F32)
    for s in range(tiles):
        table = jnp.where(lane == s, jnp.sum(acc[s], axis=1, keepdims=True), table)
    out[...] = jnp.transpose(table)[:tiles]


def add_halves(acc, s, values):
    total = values[:, :LANES]
    for j in range(1, values.shape[1] // LANES):
        total = total + values[:, j * LANES : (j + 1) * LANES]
    acc[s] += total


def prepare_kernel(
    chips, slots, even, own, target, other, mine, theirs, units, home, first, second, raw, tile, done
):
    cells = units.shape[1]
    tiles = own.shape[0] // cells
    fetch = pltpu.make_async_copy(own, raw, done.at[0])
    fetch_home = pltpu.make_async_copy(target, tile, done.at[1])
    fetch.start()
    fetch_home.start()
    members = CORES * chips
    width = members.bit_length()
    member = lax.axis_index("member")
    chip = member // CORES
    kind = odd_traced(member, width)
    counts = (jnp.int32(0), jnp.int32(0))
    for half, info in enumerate((mine, theirs)):

        def slot(k, counts, half=half, info=info):
            early, late = counts
            label = info[0, slots + k]
            w = label // CORES
            beyond = (label >= members).astype(jnp.int32)
            place = lax.rem(label, members)
            here = (odd_traced(place, width) ^ (beyond & even)) == kind
            is_late = jnp.logical_and(beyond == 1, place // CORES != chip)
            s = half * tiles + info[0, k]
            to_early = jnp.logical_and(here, jnp.logical_not(is_late))
            to_late = jnp.logical_and(here, is_late)

            @pl.when(to_early)
            def _():
                first[1 + 2 * early] = s
                first[2 + 2 * early] = w

            @pl.when(to_late)
            def _():
                second[1 + 2 * late] = s
                second[2 + 2 * late] = w

            return early + to_early.astype(jnp.int32), late + to_late.astype(jnp.int32)

        counts = lax.fori_loop(0, info[0, 2 * slots], slot, counts)
    first[0], second[0] = counts
    for s in range(tiles):
        units[tiles + s] = unit(other[s * cells : (s + 1) * cells])
    fetch.wait()
    for s in range(tiles):
        units[s] = unit(raw[s * cells : (s + 1) * cells])
    fetch_home.wait()
    home[...] = unit(tile[...])


def build_pairs(units, window, table, factors, acc, where):
    spare = acc.shape[0] - 1
    found = table[0]

    def step(m, carry):
        for i in range(GROUP):
            n = m * GROUP + i
            real = n < found
            at = jnp.where(real, n, 0)
            s, w = table[1 + 2 * at], table[2 + 2 * at]
            logits = lax.dot_general(
                units[s], window[where(w)], (((1,), (1,)), ((), ())), preferred_element_type=F32
            )
            values = jnp.exp2(logits * FACTOR)
            factors[n] = values.astype(BF16)
            add_halves(acc, jnp.where(real, s, spare), values)
        return carry

    lax.fori_loop(0, (found + GROUP - 1) // GROUP, step, 0)


def first_kernel(chips, units, table, home, *refs):
    tiles = refs[:chips]
    factors, acc, window = refs[chips:]
    chip = lax.axis_index("member") // CORES
    window[chip] = home[...]
    for k in range(1, chips):
        window[chip ^ k] = unit(tiles[k - 1][...])
    window[chips] = unit(tiles[chips - 1][...])
    acc[...] = jnp.zeros_like(acc)
    build_pairs(units, window, table, factors, acc, lambda w: jnp.minimum(w, chips))


def second_kernel(chips, units, table, before, *refs):
    tiles = refs[: chips - 1]
    factors, rows, acc, window = refs[chips - 1 :]
    chip = lax.axis_index("member") // CORES
    for k in range(1, chips):
        window[chip ^ k] = unit(tiles[k - 1][...])
    acc[...] = before[...]
    build_pairs(units, window, table, factors, acc, lambda w: w - chips)
    rows_out(acc, rows)


def row_kernel(first, second, lists_first, lists_second, columns, before, after, rows, scale, acc):
    chips = before.shape[0]
    tiles = acc.shape[0] // CORES
    scale[:chips] = float(tiles) / (columns[:chips] + before[...])
    scale[chips:] = float(tiles) / (columns[chips:] + after[...])
    acc[...] = jnp.zeros_like(acc)
    for factors, table in ((first, lists_first), (second, lists_second)):

        def pair(n, carry, factors=factors, table=table):
            s, w = table[1 + 2 * n], table[2 + 2 * n]
            add_halves(acc, s, factors[n].astype(F32) * scale[pl.ds(w, 1), :])
            return carry

        lax.fori_loop(0, table[0], pair, 0)
    rows_out(acc, rows)


def column_kernel(last, first, second, lists_first, lists_second, rows, arrived, columns, *rest):
    if last:
        logs, spread, acc = rest
    else:
        spread, acc = rest
    tiles = rows.shape[0] // CORES
    cells = first.shape[1]
    total = rows[...] + jnp.concatenate([arrived[tiles:], arrived[:tiles]], 0)
    scale = 1.0 / total
    if last:
        logs[...] = jnp.log(scale[:tiles] * float(cells))
    flipped = jnp.transpose(scale)
    for s in range(CORES * tiles):
        spread[s] = jnp.broadcast_to(flipped[:, s : s + 1], (cells, LANES))
    acc[...] = jnp.zeros_like(acc)
    for factors, table in ((first, lists_first), (second, lists_second)):

        def pair(n, carry, factors=factors, table=table):
            s, w = table[1 + 2 * n], table[2 + 2 * n]
            values = factors[n].astype(F32)
            for j in range(cells // LANES):
                part = values[:, j * LANES : (j + 1) * LANES] * spread[s]
                acc[w, :, j * LANES : (j + 1) * LANES] += jnp.sum(
                    part.reshape(cells // 8, 8, LANES), axis=0
                )
            return carry

        lax.fori_loop(0, table[0], pair, 0)
    columns[...] = jnp.sum(acc[...], axis=1)


def step(source, target, pair_source, pair_target, pair_count):
    groups, members = lax.axis_size("group"), lax.axis_size("member")
    chips = members // CORES
    cells, width = target.shape
    tiles = source.shape[0] // cells
    both = CORES * tiles
    slots = pair_source.shape[1]
    even = 1 if groups % 2 == 0 else 0
    most_first = up_to_group(min(CORES * slots, both * (chips + 1)))
    most_second = up_to_group(min(CORES * slots, both * (chips - 1)))

    beyond = hop(target, 1, 0)
    own_tiles = spread_tiles(target, chips)
    next_tiles = spread_tiles(beyond, chips)
    info = jnp.concatenate([pair_source, pair_target, pair_count[:, None]], 1)
    partner_source = partner(source)
    partner_info = partner(info)

    def shaped(*dims, kind=F32):
        return jax.ShapeDtypeStruct(dims, kind)

    def limit(size):
        return pltpu.CompilerParams(vmem_limit_bytes=int(size))

    def cost(pairs):
        return pl.CostEstimate(
            flops=2 * pairs * cells * cells * width,
            transcendentals=pairs * cells * cells,
            bytes_accessed=pairs * cells * cells * 2,
        )

    tile = cells * width * 2
    lanes_acc = (both, cells, LANES)
    prepare = pl.pallas_call(
        functools.partial(prepare_kernel, chips, slots, even),
        out_shape=(
            shaped(both, cells, width, kind=BF16),
            shaped(cells, width, kind=BF16),
            shaped(1 + 2 * most_first, kind=jnp.int32),
            shaped(1 + 2 * most_second, kind=jnp.int32),
        ),
        in_specs=[HB, HB, VM, SM, SM],
        out_specs=(VM, VM, SM, SM),
        scratch_shapes=[
            pltpu.VMEM(source.shape, BF16),
            pltpu.VMEM(target.shape, BF16),
            pltpu.SemaphoreType.DMA((2,)),
        ],
        compiler_params=limit(4 * MIB),
        cost_estimate=cost(both),
        name="prepare",
    )
    units, home, lists_first, lists_second = prepare(
        source, target, partner_source, info, partner_info
    )

    early = own_tiles[1:] + [next_tiles[0]]
    late = next_tiles[1:]
    first_call = pl.pallas_call(
        functools.partial(first_kernel, chips),
        out_shape=(shaped(most_first, cells, cells, kind=BF16), shaped(both + 1, cells, LANES)),
        in_specs=[VM, SM, VM] + [VM] * len(early),
        out_specs=(VM, VM),
        scratch_shapes=[pltpu.VMEM((chips + 1, cells, width), BF16)],
        compiler_params=limit((most_first + 2 * chips + 2 + both) * tile + 5 * MIB),
        cost_estimate=cost(most_first),
        name="first",
    )
    first, acc = first_call(units, lists_first, home, *early)
    second, rows = pl.pallas_call(
        functools.partial(second_kernel, chips),
        out_shape=(shaped(most_second, cells, cells, kind=BF16), shaped(both, cells)),
        in_specs=[VM, SM, VM] + [VM] * len(late),
        out_specs=(VM, VM),
        scratch_shapes=[
            pltpu.VMEM((both + 1, cells, LANES), F32),
            pltpu.VMEM((chips, cells, width), BF16),
        ],
        compiler_params=limit((most_second + 2 * chips + both) * tile + 5 * MIB),
        cost_estimate=cost(most_second),
        name="second",
    )(units, lists_second, acc, *late)
    held = (first, second, lists_first, lists_second)
    held_limit = limit((most_first + most_second) * tile + 4 * MIB)

    for sweep in range(ITERS):
        last = sweep + 1 == ITERS
        if sweep > 0:
            rows = pl.pallas_call(
                row_kernel,
                out_shape=shaped(both, cells),
                in_specs=[VM, VM, SM, SM, VM, VM, VM],
                out_specs=VM,
                scratch_shapes=[pltpu.VMEM((2 * chips, cells), F32), pltpu.VMEM(lanes_acc, F32)],
                compiler_params=held_limit,
                name="rows",
            )(*held, columns, before, after)
        found = pl.pallas_call(
            functools.partial(column_kernel, last),
            out_shape=(shaped(2 * chips, cells),) + ((shaped(tiles, cells),) if last else ()),
            in_specs=[VM, VM, SM, SM, VM, VM],
            out_specs=(VM,) + ((VM,) if last else ()),
            scratch_shapes=[
                pltpu.VMEM(lanes_acc, F32),
                pltpu.VMEM((2 * chips, 8, cells), F32),
            ],
            compiler_params=held_limit,
            name="columns",
        )(*held, rows, partner(rows))
        columns = found[0]
        bits = [1 << b for b in range(chips.bit_length() - 1)]
        if not last:
            for bit in bits:
                columns = columns + hop(columns, 0, bit)
            before = hop(columns[chips:], -1, 0)
            after = hop(columns[:chips], 1, 0)
        else:
            chip = lax.axis_index("member") // CORES
            for bit in bits[:-1]:
                columns = columns + hop(columns, 0, bit)
            far = bits[-1]

            def row(index):
                return lax.dynamic_slice_in_dim(columns, index, 1, 0)

            own = row(chip)
            own = own + hop(row(chip ^ far), 0, far)
            own = own + hop(row(chips + chip), -1, 0)
            own = own + hop(row(chips + (chip ^ far)), -1, far)
    return (
        found[1].reshape(tiles * cells),
        jnp.log(float(tiles) / own).reshape(cells),
    )


def solution(mesh):
    placed = (
        P(BOTH, None),
        P(BOTH, None),
        P(BOTH, None),
        P(BOTH, None),
        P(BOTH),
    )
    return jax.shard_map(
        step,
        mesh=mesh,
        in_specs=placed,
        out_specs=(P(BOTH), P(BOTH)),
        check_vma=False,
    )
```

```python
import functools
import math

import jax
import jax.numpy as jnp
from jax import lax
from jax.experimental import pallas as pl
from jax.experimental.pallas import tpu as pltpu
from jax.sharding import PartitionSpec as P


ITERS = 2
REGULARIZER = 0.05
EPSILON = 1e-06
CORES = 2
LANES = 128
MIB = 2**20
GROUP = 4
FIELD = 256


BOTH = ("group", "member")
VM = pl.BlockSpec(memory_space=pltpu.VMEM)
SM = pl.BlockSpec(memory_space=pltpu.SMEM)
F32 = jnp.float32
BF16 = jnp.bfloat16
FACTOR = math.log2(math.e) / REGULARIZER


def odd(bits):
    return bin(bits).count("1") % 2


def odd_traced(value, size):
    result = value
    for b in range(1, size.bit_length()):
        result = result ^ (value >> b)
    return result & 1


def coded(pair_source, pair_target, pair_count, members, even):
    chip = lax.axis_index("member") // CORES
    beyond = (pair_target >= members).astype(jnp.int32)
    place = pair_target - beyond * members
    kind = odd_traced(place, members) ^ (beyond & even)
    late = beyond * (place // CORES != chip).astype(jnp.int32)
    slots = pair_source.shape[1]
    listed = (jnp.arange(slots, dtype=jnp.int32)[None] < pair_count[:, None]).astype(jnp.int32)
    entry = pair_source + (pair_target // CORES) * FIELD
    code = kind + 2 * late + 4 * listed + 8 * entry
    return jnp.concatenate([code, pair_count[:, None]], 1)


def entry_of(code):
    return code & (FIELD - 1), code // FIELD


def up_to_group(count):
    return -(-count // GROUP) * GROUP


def hop(x, up, bits):
    groups, members = lax.axis_size("group"), lax.axis_size("member")
    turn = odd(bits) ^ ((up & 1) if groups % 2 == 0 else 0)
    mask = CORES * bits + turn
    return lax.ppermute(
        x,
        BOTH,
        [
            (g * members + m, (g - up) % groups * members + (m ^ mask))
            for g in range(groups)
            for m in range(members)
        ],
    )


def partner(x):
    size = lax.axis_size("member")
    return lax.ppermute(x, "member", [(i, i ^ 1) for i in range(size)])


def spread_tiles(start, chips):
    tiles = [start]
    for k in range(1, chips):
        tiles.append(hop(start, 0, k))
    return tiles


def unit(values):
    floats = values.astype(F32)
    length = jnp.sqrt(jnp.sum(floats * floats, axis=1, keepdims=True) + EPSILON)
    return (floats * (1.0 / length)).astype(BF16)


def rows_out(acc, out):
    tiles = out.shape[0]
    cells, lanes = acc.shape[1:]
    lane = lax.broadcasted_iota(jnp.int32, (cells, lanes), 1)
    table = jnp.zeros((cells, lanes), F32)
    for s in range(tiles):
        table = jnp.where(lane == s, jnp.sum(acc[s], axis=1, keepdims=True), table)
    out[...] = jnp.transpose(table)[:tiles]


def add_halves(acc, s, values):
    total = values[:, :LANES]
    for j in range(1, values.shape[1] // LANES):
        total = total + values[:, j * LANES : (j + 1) * LANES]
    acc[s] += total


def prepare_kernel(own, target, other, mine, theirs, units, home, first, second):
    cells = units.shape[1]
    tiles = own.shape[0] // cells
    slots = mine.shape[1] - 1
    kind = odd_traced(lax.axis_index("member"), lax.axis_size("member"))
    counts = (jnp.int32(0), jnp.int32(0))
    for half, info in enumerate((mine, theirs)):

        def step(m, counts, half=half, info=info):
            early, late = counts
            for i in range(math.gcd(slots, GROUP)):
                code = info[0, m * math.gcd(slots, GROUP) + i]
                hit = ((code & 5) == (4 | kind)).astype(jnp.int32)
                is_late = (code >> 1) & 1
                entry = (code >> 3) + half * tiles
                first[1 + early] = entry
                second[1 + late] = entry
                late_hit = hit & is_late
                early, late = early + hit - late_hit, late + late_hit
            return early, late

        group = math.gcd(slots, GROUP)
        counts = lax.fori_loop(0, (info[0, slots] + group - 1) // group, step, counts)
    first[0], second[0] = counts
    for s in range(tiles):
        units[s] = unit(own[s * cells : (s + 1) * cells])
        units[tiles + s] = unit(other[s * cells : (s + 1) * cells])
    home[...] = unit(target[...])


def build_pairs(units, window, table, factors, acc, where):
    spare = acc.shape[0] - 1
    found = table[0]

    def step(m, carry):
        for i in range(GROUP):
            n = m * GROUP + i
            real = n < found
            at = jnp.where(real, n, 0)
            s, w = entry_of(table[1 + at])
            logits = lax.dot_general(
                units[s], window[where(w)], (((1,), (1,)), ((), ())), preferred_element_type=F32
            )
            values = jnp.exp2(logits * FACTOR)
            factors[n] = values.astype(BF16)
            add_halves(acc, jnp.where(real, s, spare), values)
        return carry

    lax.fori_loop(0, (found + GROUP - 1) // GROUP, step, 0)


def first_kernel(chips, units, table, home, *refs):
    tiles = refs[:chips]
    factors, acc, window = refs[chips:]
    chip = lax.axis_index("member") // CORES
    window[chip] = home[...]
    for k in range(1, chips):
        window[chip ^ k] = unit(tiles[k - 1][...])
    window[chips] = unit(tiles[chips - 1][...])
    acc[...] = jnp.zeros_like(acc)
    build_pairs(units, window, table, factors, acc, lambda w: jnp.minimum(w, chips))


def second_kernel(chips, units, table, before, *refs):
    tiles = refs[: chips - 1]
    factors, rows, acc, window = refs[chips - 1 :]
    chip = lax.axis_index("member") // CORES
    for k in range(1, chips):
        window[chip ^ k] = unit(tiles[k - 1][...])
    acc[...] = before[...]
    build_pairs(units, window, table, factors, acc, lambda w: w - chips)
    rows_out(acc, rows)


def row_kernel(first, second, lists_first, lists_second, columns, before, after, rows, scale, acc):
    chips = before.shape[0]
    tiles = acc.shape[0] // CORES
    scale[:chips] = float(tiles) / (columns[:chips] + before[...])
    scale[chips:] = float(tiles) / (columns[chips:] + after[...])
    acc[...] = jnp.zeros_like(acc)
    for factors, table in ((first, lists_first), (second, lists_second)):

        def pair(n, carry, factors=factors, table=table):
            s, w = entry_of(table[1 + n])
            add_halves(acc, s, factors[n].astype(F32) * scale[pl.ds(w, 1), :])
            return carry

        lax.fori_loop(0, table[0], pair, 0)
    rows_out(acc, rows)


def column_kernel(last, first, second, lists_first, lists_second, rows, arrived, columns, *rest):
    if last:
        logs, spread, acc = rest
    else:
        spread, acc = rest
    tiles = rows.shape[0] // CORES
    cells = first.shape[1]
    total = rows[...] + jnp.concatenate([arrived[tiles:], arrived[:tiles]], 0)
    scale = 1.0 / total
    if last:
        logs[...] = jnp.log(scale[:tiles] * float(cells))
    for s in range(CORES * tiles):
        spread[s] = jnp.transpose(jnp.broadcast_to(scale[s : s + 1], (LANES, cells)))
    acc[...] = jnp.zeros_like(acc)
    spare = acc.shape[0] - 1
    for factors, table in ((first, lists_first), (second, lists_second)):
        found = table[0]

        def step(m, carry, factors=factors, table=table, found=found):
            for i in range(GROUP):
                n = m * GROUP + i
                real = n < found
                s, w = entry_of(table[1 + jnp.where(real, n, 0)])
                w = jnp.where(real, w, spare)
                values = factors[n].astype(F32)
                for j in range(cells // LANES):
                    part = values[:, j * LANES : (j + 1) * LANES] * spread[s]
                    acc[w, :, j * LANES : (j + 1) * LANES] += jnp.sum(
                        part.reshape(cells // 8, 8, LANES), axis=0
                    )
            return carry

        lax.fori_loop(0, (found + GROUP - 1) // GROUP, step, 0)
    columns[...] = jnp.sum(acc[:spare], axis=1)


def step(source, target, pair_source, pair_target, pair_count):
    groups, members = lax.axis_size("group"), lax.axis_size("member")
    chips = members // CORES
    cells, width = target.shape
    tiles = source.shape[0] // cells
    both = CORES * tiles
    slots = pair_source.shape[1]
    even = 1 if groups % 2 == 0 else 0
    most_first = up_to_group(min(CORES * slots, both * (chips + 1)))
    most_second = up_to_group(min(CORES * slots, both * (chips - 1)))

    beyond = hop(target, 1, 0)
    own_tiles = spread_tiles(target, chips)
    next_tiles = spread_tiles(beyond, chips)
    info = coded(pair_source, pair_target, pair_count, members, even)
    partner_source = partner(source)
    stay = [(i, i) for i in range(members)]
    own_source = lax.ppermute(source, "member", stay)
    own_target = lax.ppermute(target, "member", stay)
    partner_info = partner(info)

    def shaped(*dims, kind=F32):
        return jax.ShapeDtypeStruct(dims, kind)

    def limit(size):
        return pltpu.CompilerParams(vmem_limit_bytes=int(size))

    def cost(pairs):
        return pl.CostEstimate(
            flops=2 * pairs * cells * cells * width,
            transcendentals=pairs * cells * cells,
            bytes_accessed=pairs * cells * cells * 2,
        )

    tile = cells * width * 2
    lanes_acc = (both, cells, LANES)
    prepare = pl.pallas_call(
        prepare_kernel,
        out_shape=(
            shaped(both, cells, width, kind=BF16),
            shaped(cells, width, kind=BF16),
            shaped(2 + most_first, kind=jnp.int32),
            shaped(2 + most_second, kind=jnp.int32),
        ),
        in_specs=[VM, VM, VM, SM, SM],
        out_specs=(VM, VM, SM, SM),
        compiler_params=limit(4 * MIB),
        cost_estimate=cost(both),
        name="prepare",
    )
    units, home, lists_first, lists_second = prepare(
        own_source, own_target, partner_source, info, partner_info
    )

    early = own_tiles[1:] + [next_tiles[0]]
    late = next_tiles[1:]
    first_call = pl.pallas_call(
        functools.partial(first_kernel, chips),
        out_shape=(shaped(most_first, cells, cells, kind=BF16), shaped(both + 1, cells, LANES)),
        in_specs=[VM, SM, VM] + [VM] * len(early),
        out_specs=(VM, VM),
        scratch_shapes=[pltpu.VMEM((chips + 1, cells, width), BF16)],
        compiler_params=limit((most_first + 2 * chips + 2 + both) * tile + 5 * MIB),
        cost_estimate=cost(most_first),
        name="first",
    )
    first, acc = first_call(units, lists_first, home, *early)
    second, rows = pl.pallas_call(
        functools.partial(second_kernel, chips),
        out_shape=(shaped(most_second, cells, cells, kind=BF16), shaped(both, cells)),
        in_specs=[VM, SM, VM] + [VM] * len(late),
        out_specs=(VM, VM),
        scratch_shapes=[
            pltpu.VMEM((both + 1, cells, LANES), F32),
            pltpu.VMEM((chips, cells, width), BF16),
        ],
        compiler_params=limit((most_second + 2 * chips + both) * tile + 5 * MIB),
        cost_estimate=cost(most_second),
        name="second",
    )(units, lists_second, acc, *late)
    held = (first, second, lists_first, lists_second)
    held_limit = limit((most_first + most_second) * tile + 4 * MIB)

    for sweep in range(ITERS):
        last = sweep + 1 == ITERS
        if sweep > 0:
            rows = pl.pallas_call(
                row_kernel,
                out_shape=shaped(both, cells),
                in_specs=[VM, VM, SM, SM, VM, VM, VM],
                out_specs=VM,
                scratch_shapes=[pltpu.VMEM((2 * chips, cells), F32), pltpu.VMEM(lanes_acc, F32)],
                compiler_params=held_limit,
                name="rows",
            )(*held, columns, before, after)
        found = pl.pallas_call(
            functools.partial(column_kernel, last),
            out_shape=(shaped(2 * chips, cells),) + ((shaped(tiles, cells),) if last else ()),
            in_specs=[VM, VM, SM, SM, VM, VM],
            out_specs=(VM,) + ((VM,) if last else ()),
            scratch_shapes=[
                pltpu.VMEM(lanes_acc, F32),
                pltpu.VMEM((2 * chips + 1, 8, cells), F32),
            ],
            compiler_params=held_limit,
            name="columns",
        )(*held, rows, partner(rows))
        columns = found[0]
        bits = [1 << b for b in range(chips.bit_length() - 1)]
        if not last:
            for bit in bits:
                columns = columns + hop(columns, 0, bit)
            before = hop(columns[chips:], -1, 0)
            after = hop(columns[:chips], 1, 0)
        else:
            chip = lax.axis_index("member") // CORES
            for bit in bits[:-1]:
                columns = columns + hop(columns, 0, bit)
            far = bits[-1]

            def row(index):
                return lax.dynamic_slice_in_dim(columns, index, 1, 0)

            own = row(chip)
            own = own + hop(row(chip ^ far), 0, far)
            own = own + hop(row(chips + chip), -1, 0)
            own = own + hop(row(chips + (chip ^ far)), -1, far)
    return (
        found[1].reshape(tiles * cells),
        jnp.log(float(tiles) / own).reshape(cells),
    )


def solution(mesh):
    placed = (
        P(BOTH, None),
        P(BOTH, None),
        P(BOTH, None),
        P(BOTH, None),
        P(BOTH),
    )
    return jax.shard_map(
        step,
        mesh=mesh,
        in_specs=placed,
        out_specs=(P(BOTH), P(BOTH)),
        check_vma=False,
    )
```

```python
import functools
import math

import jax
import jax.numpy as jnp
from jax import lax
from jax.experimental import pallas as pl
from jax.experimental.pallas import tpu as pltpu
from jax.sharding import PartitionSpec as P


ITERS = 2
REGULARIZER = 0.05
EPSILON = 1e-06
CORES = 2
LANES = 128
MIB = 2**20
GROUP = 4
FIELD = 256
STRAIGHT = {3: 8}


BOTH = ("group", "member")
VM = pl.BlockSpec(memory_space=pltpu.VMEM)
SM = pl.BlockSpec(memory_space=pltpu.SMEM)
F32 = jnp.float32
BF16 = jnp.bfloat16
FACTOR = math.log2(math.e) / REGULARIZER


def odd(bits):
    return bin(bits).count("1") % 2


def odd_traced(value, size):
    result = value
    for b in range(1, size.bit_length()):
        result = result ^ (value >> b)
    return result & 1


def coded(pair_source, pair_target, pair_count, members, even):
    chip = lax.axis_index("member") // CORES
    beyond = (pair_target >= members).astype(jnp.int32)
    place = pair_target - beyond * members
    kind = odd_traced(place, members) ^ (beyond & even)
    late = beyond * (place // CORES != chip).astype(jnp.int32)
    slots = pair_source.shape[1]
    listed = (jnp.arange(slots, dtype=jnp.int32)[None] < pair_count[:, None]).astype(jnp.int32)
    entry = pair_source + (pair_target // CORES) * FIELD
    code = kind + 2 * late + 4 * listed + 8 * entry
    return jnp.concatenate([code, pair_count[:, None]], 1)


def entry_of(code):
    return code & (FIELD - 1), code // FIELD


def up_to_group(count):
    return -(-count // GROUP) * GROUP


def hop(x, up, bits):
    groups, members = lax.axis_size("group"), lax.axis_size("member")
    turn = odd(bits) ^ ((up & 1) if groups % 2 == 0 else 0)
    mask = CORES * bits + turn
    return lax.ppermute(
        x,
        BOTH,
        [
            (g * members + m, (g - up) % groups * members + (m ^ mask))
            for g in range(groups)
            for m in range(members)
        ],
    )


def pair_groups(x, odd_first):
    groups, members = lax.axis_size("group"), lax.axis_size("member")
    pairs = []
    for g in range(groups):
        other = (g + (1 if (g % 2 == 1) == odd_first else -1)) % groups
        pairs += [(g * members + m, other * members + (m ^ 1)) for m in range(members)]
    return lax.ppermute(x, BOTH, pairs)


def partner(x):
    size = lax.axis_size("member")
    return lax.ppermute(x, "member", [(i, i ^ 1) for i in range(size)])


def plan_of(chips):
    return {k: STRAIGHT.get(k, 0) for k in range(1, chips)}


def gathered(target, beyond, chips):
    own = []
    for k in range(1, chips):
        own.append(hop(target, 0, k))
    blocks = {}
    for k, eighths in plan_of(chips).items():
        cut = target.shape[0] * eighths // 8
        blocks[k] = []
        if cut > 0:
            blocks[k].append(hop(target[:cut], 1, k))
        if cut < target.shape[0]:
            blocks[k].append(hop(beyond[cut:], 0, k))
    return own, [blocks[k] for k in range(1, chips)]


def place(window, at, blocks):
    row = 0
    for block in blocks:
        rows = block.shape[0]
        window[at, row : row + rows] = unit(block[...])
        row += rows


def unit(values):
    floats = values.astype(F32)
    length = jnp.sqrt(jnp.sum(floats * floats, axis=1, keepdims=True) + EPSILON)
    return (floats * (1.0 / length)).astype(BF16)


def rows_out(acc, out):
    tiles = out.shape[0]
    cells, lanes = acc.shape[1:]
    lane = lax.broadcasted_iota(jnp.int32, (cells, lanes), 1)
    table = jnp.zeros((cells, lanes), F32)
    for s in range(tiles):
        table = jnp.where(lane == s, jnp.sum(acc[s], axis=1, keepdims=True), table)
    out[...] = jnp.transpose(table)[:tiles]


def add_halves(acc, s, values):
    total = values[:, :LANES]
    for j in range(1, values.shape[1] // LANES):
        total = total + values[:, j * LANES : (j + 1) * LANES]
    acc[s] += total


def prepare_kernel(own, target, other, mine, theirs, units, home, first, second):
    cells = units.shape[1]
    tiles = own.shape[0] // cells
    slots = mine.shape[1] - 1
    kind = odd_traced(lax.axis_index("member"), lax.axis_size("member"))
    counts = (jnp.int32(0), jnp.int32(0))
    for half, info in enumerate((mine, theirs)):

        def step(m, counts, half=half, info=info):
            early, late = counts
            for i in range(math.gcd(slots, GROUP)):
                code = info[0, m * math.gcd(slots, GROUP) + i]
                hit = ((code & 5) == (4 | kind)).astype(jnp.int32)
                is_late = (code >> 1) & 1
                entry = (code >> 3) + half * tiles
                first[1 + early] = entry
                second[1 + late] = entry
                late_hit = hit & is_late
                early, late = early + hit - late_hit, late + late_hit
            return early, late

        group = math.gcd(slots, GROUP)
        counts = lax.fori_loop(0, (info[0, slots] + group - 1) // group, step, counts)
    first[0], second[0] = counts
    for s in range(tiles):
        units[s] = unit(own[s * cells : (s + 1) * cells])
        units[tiles + s] = unit(other[s * cells : (s + 1) * cells])
    home[...] = unit(target[...])


def build_pairs(units, window, table, factors, acc, where):
    spare = acc.shape[0] - 1
    found = table[0]

    def step(m, carry):
        for i in range(GROUP):
            n = m * GROUP + i
            real = n < found
            at = jnp.where(real, n, 0)
            s, w = entry_of(table[1 + at])
            logits = lax.dot_general(
                units[s], window[where(w)], (((1,), (1,)), ((), ())), preferred_element_type=F32
            )
            values = jnp.exp2(logits * FACTOR)
            factors[n] = values.astype(BF16)
            add_halves(acc, jnp.where(real, s, spare), values)
        return carry

    lax.fori_loop(0, (found + GROUP - 1) // GROUP, step, 0)


def first_kernel(chips, units, table, home, *refs):
    tiles = refs[:chips]
    factors, acc, window = refs[chips:]
    chip = lax.axis_index("member") // CORES
    window[chip] = home[...]
    for k in range(1, chips):
        window[chip ^ k] = unit(tiles[k - 1][...])
    window[chips] = unit(tiles[chips - 1][...])
    acc[...] = jnp.zeros_like(acc)
    build_pairs(units, window, table, factors, acc, lambda w: jnp.minimum(w, chips))


def second_kernel(shape, units, table, before, *refs):
    chips = len(shape) + 1
    tiles = list(refs[: sum(shape)])
    factors, rows, acc, window = refs[sum(shape) :]
    chip = lax.axis_index("member") // CORES
    for k, count in enumerate(shape):
        place(window, chip ^ (k + 1), [tiles.pop(0) for _ in range(count)])
    acc[...] = before[...]
    build_pairs(units, window, table, factors, acc, lambda w: w - chips)
    rows_out(acc, rows)


def row_kernel(
    paired, first, second, lists_first, lists_second, columns, wide, near, rows, scale, acc
):
    chips = columns.shape[0] // 2
    tiles = acc.shape[0] // CORES
    below, above = wide[...], near[...]
    if paired:
        swapped = (lax.axis_index("group") & 1) == 1
        below, above = jnp.where(swapped, above, below), jnp.where(swapped, below, above)
    scale[:chips] = float(tiles) / (columns[:chips] + below[chips:])
    scale[chips:] = float(tiles) / (columns[chips:] + above[:chips])
    acc[...] = jnp.zeros_like(acc)
    for factors, table in ((first, lists_first), (second, lists_second)):

        def pair(n, carry, factors=factors, table=table):
            s, w = entry_of(table[1 + n])
            add_halves(acc, s, factors[n].astype(F32) * scale[pl.ds(w, 1), :])
            return carry

        lax.fori_loop(0, table[0], pair, 0)
    rows_out(acc, rows)


def column_kernel(last, first, second, lists_first, lists_second, rows, arrived, columns, *rest):
    if last:
        logs, spread, acc = rest
    else:
        spread, acc = rest
    tiles = rows.shape[0] // CORES
    cells = first.shape[1]
    total = rows[...] + jnp.concatenate([arrived[tiles:], arrived[:tiles]], 0)
    scale = 1.0 / total
    if last:
        logs[...] = jnp.log(scale[:tiles] * float(cells))
    for s in range(CORES * tiles):
        spread[s] = jnp.transpose(jnp.broadcast_to(scale[s : s + 1], (LANES, cells)))
    acc[...] = jnp.zeros_like(acc)
    spare = acc.shape[0] - 1
    for factors, table in ((first, lists_first), (second, lists_second)):
        found = table[0]

        def step(m, carry, factors=factors, table=table, found=found):
            for i in range(GROUP):
                n = m * GROUP + i
                real = n < found
                s, w = entry_of(table[1 + jnp.where(real, n, 0)])
                w = jnp.where(real, w, spare)
                values = factors[n].astype(F32)
                for j in range(cells // LANES):
                    part = values[:, j * LANES : (j + 1) * LANES] * spread[s]
                    acc[w, :, j * LANES : (j + 1) * LANES] += jnp.sum(
                        part.reshape(cells // 8, 8, LANES), axis=0
                    )
            return carry

        lax.fori_loop(0, (found + GROUP - 1) // GROUP, step, 0)
    columns[...] = jnp.sum(acc[:spare], axis=1)


def step(source, target, pair_source, pair_target, pair_count):
    groups, members = lax.axis_size("group"), lax.axis_size("member")
    chips = members // CORES
    cells, width = target.shape
    tiles = source.shape[0] // cells
    both = CORES * tiles
    slots = pair_source.shape[1]
    even = 1 if groups % 2 == 0 else 0
    most_first = up_to_group(min(CORES * slots, both * (chips + 1)))
    most_second = up_to_group(min(CORES * slots, both * (chips - 1)))

    beyond = hop(target, 1, 0)
    own_tiles, next_tiles = gathered(target, beyond, chips)
    info = coded(pair_source, pair_target, pair_count, members, even)
    partner_source = partner(source)
    stay = [(i, i) for i in range(members)]
    own_source = lax.ppermute(source, "member", stay)
    own_target = lax.ppermute(target, "member", stay)
    partner_info = partner(info)

    def shaped(*dims, kind=F32):
        return jax.ShapeDtypeStruct(dims, kind)

    def limit(size):
        return pltpu.CompilerParams(vmem_limit_bytes=int(size))

    def cost(pairs):
        return pl.CostEstimate(
            flops=2 * pairs * cells * cells * width,
            transcendentals=pairs * cells * cells,
            bytes_accessed=pairs * cells * cells * 2,
        )

    tile = cells * width * 2
    lanes_acc = (both, cells, LANES)
    prepare = pl.pallas_call(
        prepare_kernel,
        out_shape=(
            shaped(both, cells, width, kind=BF16),
            shaped(cells, width, kind=BF16),
            shaped(2 + most_first, kind=jnp.int32),
            shaped(2 + most_second, kind=jnp.int32),
        ),
        in_specs=[VM, VM, VM, SM, SM],
        out_specs=(VM, VM, SM, SM),
        compiler_params=limit(4 * MIB),
        cost_estimate=cost(both),
        name="prepare",
    )
    units, home, lists_first, lists_second = prepare(
        own_source, own_target, partner_source, info, partner_info
    )

    early = own_tiles + [beyond]
    late = [block for blocks in next_tiles for block in blocks]
    first_call = pl.pallas_call(
        functools.partial(first_kernel, chips),
        out_shape=(shaped(most_first, cells, cells, kind=BF16), shaped(both + 1, cells, LANES)),
        in_specs=[VM, SM, VM] + [VM] * len(early),
        out_specs=(VM, VM),
        scratch_shapes=[pltpu.VMEM((chips + 1, cells, width), BF16)],
        compiler_params=limit((most_first + 2 * chips + 2 + both) * tile + 5 * MIB),
        cost_estimate=cost(most_first),
        name="first",
    )
    first, acc = first_call(units, lists_first, home, *early)
    second, rows = pl.pallas_call(
        functools.partial(second_kernel, [len(blocks) for blocks in next_tiles]),
        out_shape=(shaped(most_second, cells, cells, kind=BF16), shaped(both, cells)),
        in_specs=[VM, SM, VM] + [VM] * len(late),
        out_specs=(VM, VM),
        scratch_shapes=[
            pltpu.VMEM((both + 1, cells, LANES), F32),
            pltpu.VMEM((chips, cells, width), BF16),
        ],
        compiler_params=limit((most_second + 2 * chips + both) * tile + 5 * MIB),
        cost_estimate=cost(most_second),
        name="second",
    )(units, lists_second, acc, *late)
    held = (first, second, lists_first, lists_second)
    held_limit = limit((most_first + most_second) * tile + 4 * MIB)

    for sweep in range(ITERS):
        last = sweep + 1 == ITERS
        if sweep > 0:
            rows = pl.pallas_call(
                functools.partial(row_kernel, even == 1),
                out_shape=shaped(both, cells),
                in_specs=[VM, VM, SM, SM, VM, VM, VM],
                out_specs=VM,
                scratch_shapes=[pltpu.VMEM((2 * chips, cells), F32), pltpu.VMEM(lanes_acc, F32)],
                compiler_params=held_limit,
                name="rows",
            )(*held, columns, wide, near)
        found = pl.pallas_call(
            functools.partial(column_kernel, last),
            out_shape=(shaped(2 * chips, cells),) + ((shaped(tiles, cells),) if last else ()),
            in_specs=[VM, VM, SM, SM, VM, VM],
            out_specs=(VM,) + ((VM,) if last else ()),
            scratch_shapes=[
                pltpu.VMEM(lanes_acc, F32),
                pltpu.VMEM((2 * chips + 1, 8, cells), F32),
            ],
            compiler_params=held_limit,
            name="columns",
        )(*held, rows, partner(rows))
        columns = found[0]
        bits = [1 << b for b in range(chips.bit_length() - 1)]
        if not last:
            for bit in bits:
                columns = columns + hop(columns, 0, bit)
            wide = pair_groups(columns, True) if even else hop(columns, -1, 0)
            near = pair_groups(columns, False) if even else hop(columns, 1, 0)
        else:
            chip = lax.axis_index("member") // CORES
            for bit in bits[:-1]:
                columns = columns + hop(columns, 0, bit)
            far = bits[-1]

            def row(index):
                return lax.dynamic_slice_in_dim(columns, index, 1, 0)

            own = row(chip)
            own = own + hop(row(chip ^ far), 0, far)
            own = own + hop(row(chips + chip), -1, 0)
            own = own + hop(row(chips + (chip ^ far)), -1, far)
    return (
        found[1].reshape(tiles * cells),
        jnp.log(float(tiles) / own).reshape(cells),
    )


def solution(mesh):
    placed = (
        P(BOTH, None),
        P(BOTH, None),
        P(BOTH, None),
        P(BOTH, None),
        P(BOTH),
    )
    return jax.shard_map(
        step,
        mesh=mesh,
        in_specs=placed,
        out_specs=(P(BOTH), P(BOTH)),
        check_vma=False,
    )
```

```python
import functools
import math

import jax
import jax.numpy as jnp
from jax import lax
from jax.experimental import pallas as pl
from jax.experimental.pallas import tpu as pltpu
from jax.sharding import PartitionSpec as P


ITERS = 2
REGULARIZER = 0.05
EPSILON = 1e-06
CORES = 2
LANES = 128
MIB = 2**20
GROUP = 4
FIELD = 256
STRAIGHT = {3: 8}


BOTH = ("group", "member")
VM = pl.BlockSpec(memory_space=pltpu.VMEM)
SM = pl.BlockSpec(memory_space=pltpu.SMEM)
F32 = jnp.float32
BF16 = jnp.bfloat16
FACTOR = math.log2(math.e) / REGULARIZER


def odd(bits):
    return bin(bits).count("1") % 2


def odd_traced(value, size):
    result = value
    for b in range(1, size.bit_length()):
        result = result ^ (value >> b)
    return result & 1


def coded(pair_source, pair_target, pair_count, members, even):
    chip = lax.axis_index("member") // CORES
    beyond = (pair_target >= members).astype(jnp.int32)
    place = pair_target - beyond * members
    kind = odd_traced(place, members) ^ (beyond & even)
    late = beyond * (place // CORES != chip).astype(jnp.int32)
    slots = pair_source.shape[1]
    listed = (jnp.arange(slots, dtype=jnp.int32)[None] < pair_count[:, None]).astype(jnp.int32)
    entry = pair_source + (pair_target // CORES) * FIELD
    code = kind + 2 * late + 4 * listed + 8 * entry
    return jnp.concatenate([code, pair_count[:, None]], 1)


def entry_of(code):
    return code & (FIELD - 1), code // FIELD


def up_to_group(count):
    return -(-count // GROUP) * GROUP


def hop(x, up, bits):
    groups, members = lax.axis_size("group"), lax.axis_size("member")
    turn = odd(bits) ^ ((up & 1) if groups % 2 == 0 else 0)
    mask = CORES * bits + turn
    return lax.ppermute(
        x,
        BOTH,
        [
            (g * members + m, (g - up) % groups * members + (m ^ mask))
            for g in range(groups)
            for m in range(members)
        ],
    )


def pair_groups(x, odd_first):
    groups, members = lax.axis_size("group"), lax.axis_size("member")
    pairs = []
    for g in range(groups):
        other = (g + (1 if (g % 2 == 1) == odd_first else -1)) % groups
        pairs += [(g * members + m, other * members + (m ^ 1)) for m in range(members)]
    return lax.ppermute(x, BOTH, pairs)


def partner(x):
    size = lax.axis_size("member")
    return lax.ppermute(x, "member", [(i, i ^ 1) for i in range(size)])


def plan_of(chips):
    return {k: STRAIGHT.get(k, 0) for k in range(1, chips)}


def gathered(target, beyond, chips):
    own = []
    for k in range(1, chips):
        own.append(hop(target, 0, k))
    blocks = {}
    for k, eighths in plan_of(chips).items():
        cut = target.shape[0] * eighths // 8
        blocks[k] = []
        if cut > 0:
            blocks[k].append(hop(target[:cut], 1, k))
        if cut < target.shape[0]:
            blocks[k].append(hop(beyond[cut:], 0, k))
    return own, [blocks[k] for k in range(1, chips)]


def place(window, at, blocks):
    row = 0
    for block in blocks:
        rows = block.shape[0]
        window[at, row : row + rows] = unit(block[...])
        row += rows


def unit(values):
    floats = values.astype(F32)
    length = jnp.sqrt(jnp.sum(floats * floats, axis=1, keepdims=True) + EPSILON)
    return (floats * (1.0 / length)).astype(BF16)


def rows_out(acc, out):
    tiles = out.shape[0]
    cells, lanes = acc.shape[1:]
    lane = lax.broadcasted_iota(jnp.int32, (cells, lanes), 1)
    table = jnp.zeros((cells, lanes), F32)
    for s in range(tiles):
        table = jnp.where(lane == s, jnp.sum(acc[s], axis=1, keepdims=True), table)
    out[...] = jnp.transpose(table)[:tiles]


def add_halves(acc, s, values):
    total = values[:, :LANES]
    for j in range(1, values.shape[1] // LANES):
        total = total + values[:, j * LANES : (j + 1) * LANES]
    acc[s] += total


def prepare_kernel(own, target, other, mine, theirs, units, home, first, second):
    cells = units.shape[1]
    tiles = own.shape[0] // cells
    slots = mine.shape[1] - 1
    kind = odd_traced(lax.axis_index("member"), lax.axis_size("member"))
    counts = (jnp.int32(0), jnp.int32(0))
    for half, info in enumerate((mine, theirs)):

        def step(m, counts, half=half, info=info):
            early, late = counts
            for i in range(math.gcd(slots, GROUP)):
                code = info[0, m * math.gcd(slots, GROUP) + i]
                hit = ((code & 5) == (4 | kind)).astype(jnp.int32)
                is_late = (code >> 1) & 1
                entry = (code >> 3) + half * tiles
                first[1 + early] = entry
                second[1 + late] = entry
                late_hit = hit & is_late
                early, late = early + hit - late_hit, late + late_hit
            return early, late

        group = math.gcd(slots, GROUP)
        counts = lax.fori_loop(0, (info[0, slots] + group - 1) // group, step, counts)
    first[0], second[0] = counts
    for s in range(tiles):
        units[s] = unit(own[s * cells : (s + 1) * cells])
        units[tiles + s] = unit(other[s * cells : (s + 1) * cells])
    home[...] = unit(target[...])


def build_pairs(units, window, table, factors, acc, where):
    spare = acc.shape[0] - 1
    found = table[0]

    def step(m, carry):
        for i in range(GROUP):
            n = m * GROUP + i
            real = n < found
            at = jnp.where(real, n, 0)
            s, w = entry_of(table[1 + at])
            logits = lax.dot_general(
                units[s], window[where(w)], (((1,), (1,)), ((), ())), preferred_element_type=F32
            )
            values = jnp.exp2(logits * FACTOR)
            factors[n] = values.astype(BF16)
            add_halves(acc, jnp.where(real, s, spare), values)
        return carry

    lax.fori_loop(0, (found + GROUP - 1) // GROUP, step, 0)


def first_kernel(chips, units, table, home, *refs):
    tiles = refs[:chips]
    factors, acc, window = refs[chips:]
    chip = lax.axis_index("member") // CORES
    window[chip] = home[...]
    for k in range(1, chips):
        window[chip ^ k] = unit(tiles[k - 1][...])
    window[chips] = unit(tiles[chips - 1][...])
    acc[...] = jnp.zeros_like(acc)
    build_pairs(units, window, table, factors, acc, lambda w: jnp.minimum(w, chips))


def second_kernel(shape, units, table, before, *refs):
    chips = len(shape) + 1
    tiles = list(refs[: sum(shape)])
    factors, rows, acc, window = refs[sum(shape) :]
    chip = lax.axis_index("member") // CORES
    for k, count in enumerate(shape):
        place(window, chip ^ (k + 1), [tiles.pop(0) for _ in range(count)])
    acc[...] = before[...]
    build_pairs(units, window, table, factors, acc, lambda w: w - chips)
    rows_out(acc, rows)


def row_kernel(
    paired, first, second, lists_first, lists_second, columns, wide, near, rows, scale, acc
):
    chips = columns.shape[0] // 2
    tiles = acc.shape[0] // CORES
    below, above = wide[...], near[...]
    if paired:
        swapped = (lax.axis_index("group") & 1) == 1
        below, above = jnp.where(swapped, above, below), jnp.where(swapped, below, above)
    scale[:chips] = float(tiles) / (columns[:chips] + below[chips:])
    scale[chips:] = float(tiles) / (columns[chips:] + above[:chips])
    acc[...] = jnp.zeros_like(acc)
    for factors, table in ((first, lists_first), (second, lists_second)):

        def pair(n, carry, factors=factors, table=table):
            s, w = entry_of(table[1 + n])
            add_halves(acc, s, factors[n].astype(F32) * scale[pl.ds(w, 1), :])
            return carry

        lax.fori_loop(0, table[0], pair, 0)
    rows_out(acc, rows)


def column_kernel(last, first, second, lists_first, lists_second, rows, arrived, columns, *rest):
    if last:
        logs, spread, acc = rest
    else:
        spread, acc = rest
    tiles = rows.shape[0] // CORES
    cells = first.shape[1]
    total = rows[...] + jnp.concatenate([arrived[tiles:], arrived[:tiles]], 0)
    scale = 1.0 / total
    if last:
        logs[...] = jnp.log(scale[:tiles] * float(cells))
    for s in range(CORES * tiles):
        spread[s] = jnp.transpose(jnp.broadcast_to(scale[s : s + 1], (LANES, cells)))
    acc[...] = jnp.zeros_like(acc)
    spare = acc.shape[0] - 1
    for factors, table in ((first, lists_first), (second, lists_second)):
        found = table[0]

        def step(m, carry, factors=factors, table=table, found=found):
            for i in range(GROUP):
                n = m * GROUP + i
                real = n < found
                s, w = entry_of(table[1 + jnp.where(real, n, 0)])
                w = jnp.where(real, w, spare)
                values = factors[n].astype(F32)
                for j in range(cells // LANES):
                    part = values[:, j * LANES : (j + 1) * LANES] * spread[s]
                    acc[w, :, j * LANES : (j + 1) * LANES] += jnp.sum(
                        part.reshape(cells // 8, 8, LANES), axis=0
                    )
            return carry

        lax.fori_loop(0, (found + GROUP - 1) // GROUP, step, 0)
    columns[...] = jnp.sum(acc[:spare], axis=1)


def step(source, target, pair_source, pair_target, pair_count):
    groups, members = lax.axis_size("group"), lax.axis_size("member")
    chips = members // CORES
    cells, width = target.shape
    tiles = source.shape[0] // cells
    both = CORES * tiles
    slots = pair_source.shape[1]
    even = 1 if groups % 2 == 0 else 0
    most_first = up_to_group(min(CORES * slots, both * (chips + 1)))
    most_second = up_to_group(min(CORES * slots, both * (chips - 1)))

    beyond = hop(target, 1, 0)
    own_tiles, next_tiles = gathered(target, beyond, chips)
    info = coded(pair_source, pair_target, pair_count, members, even)
    partner_source = partner(source)
    stay = [(i, i) for i in range(members)]
    own_source = lax.ppermute(source, "member", stay)
    own_target = lax.ppermute(target, "member", stay)
    partner_info = partner(info)

    def shaped(*dims, kind=F32):
        return jax.ShapeDtypeStruct(dims, kind)

    def limit(size):
        return pltpu.CompilerParams(vmem_limit_bytes=int(size))

    def cost(pairs):
        return pl.CostEstimate(
            flops=2 * pairs * cells * cells * width,
            transcendentals=pairs * cells * cells,
            bytes_accessed=pairs * cells * cells * 2,
        )

    tile = cells * width * 2
    lanes_acc = (both, cells, LANES)
    prepare = pl.pallas_call(
        prepare_kernel,
        out_shape=(
            shaped(both, cells, width, kind=BF16),
            shaped(cells, width, kind=BF16),
            shaped(2 + most_first, kind=jnp.int32),
            shaped(2 + most_second, kind=jnp.int32),
        ),
        in_specs=[VM, VM, VM, SM, SM],
        out_specs=(VM, VM, SM, SM),
        compiler_params=limit(4 * MIB),
        cost_estimate=cost(both),
        name="prepare",
    )
    units, home, lists_first, lists_second = prepare(
        own_source, own_target, partner_source, info, partner_info
    )

    early = own_tiles + [beyond]
    late = [block for blocks in next_tiles for block in blocks]
    first_call = pl.pallas_call(
        functools.partial(first_kernel, chips),
        out_shape=(shaped(most_first, cells, cells, kind=BF16), shaped(both + 1, cells, LANES)),
        in_specs=[VM, SM, VM] + [VM] * len(early),
        out_specs=(VM, VM),
        scratch_shapes=[pltpu.VMEM((chips + 1, cells, width), BF16)],
        compiler_params=limit((most_first + 2 * chips + 2 + both) * tile + 5 * MIB),
        cost_estimate=cost(most_first),
        name="first",
    )
    first, acc = first_call(units, lists_first, home, *early)
    second, rows = pl.pallas_call(
        functools.partial(second_kernel, [len(blocks) for blocks in next_tiles]),
        out_shape=(shaped(most_second, cells, cells, kind=BF16), shaped(both, cells)),
        in_specs=[VM, SM, VM] + [VM] * len(late),
        out_specs=(VM, VM),
        scratch_shapes=[
            pltpu.VMEM((both + 1, cells, LANES), F32),
            pltpu.VMEM((chips, cells, width), BF16),
        ],
        compiler_params=limit((most_second + 2 * chips + both) * tile + 5 * MIB),
        cost_estimate=cost(most_second),
        name="second",
    )(units, lists_second, acc, *late)
    held = (first, second, lists_first, lists_second)
    held_limit = limit((most_first + most_second) * tile + 4 * MIB)

    for sweep in range(ITERS):
        last = sweep + 1 == ITERS
        if sweep > 0:
            rows = pl.pallas_call(
                functools.partial(row_kernel, even == 1),
                out_shape=shaped(both, cells),
                in_specs=[VM, VM, SM, SM, VM, VM, VM],
                out_specs=VM,
                scratch_shapes=[pltpu.VMEM((2 * chips, cells), F32), pltpu.VMEM(lanes_acc, F32)],
                compiler_params=held_limit,
                name="rows",
            )(*held, columns, wide, near)
        found = pl.pallas_call(
            functools.partial(column_kernel, last),
            out_shape=(shaped(2 * chips, cells),) + ((shaped(tiles, cells),) if last else ()),
            in_specs=[VM, VM, SM, SM, VM, VM],
            out_specs=(VM,) + ((VM,) if last else ()),
            scratch_shapes=[
                pltpu.VMEM(lanes_acc, F32),
                pltpu.VMEM((2 * chips + 1, 8, cells), F32),
            ],
            compiler_params=held_limit,
            name="columns",
        )(*held, rows, partner(rows))
        columns = found[0]
        bits = [1 << b for b in range(chips.bit_length() - 1)]
        if not last:
            if chips == 4:
                shares = []
                for k in (3, 1, 2):
                    shares.append(hop(columns, 0, k))
                columns = columns + shares[0] + shares[1] + shares[2]
            else:
                for bit in bits:
                    columns = columns + hop(columns, 0, bit)
            wide = pair_groups(columns, True) if even else hop(columns, -1, 0)
            near = pair_groups(columns, False) if even else hop(columns, 1, 0)
        else:
            chip = lax.axis_index("member") // CORES
            for bit in bits[:-1]:
                columns = columns + hop(columns, 0, bit)
            far = bits[-1]

            def row(index):
                return lax.dynamic_slice_in_dim(columns, index, 1, 0)

            own = row(chip)
            own = own + hop(row(chip ^ far), 0, far)
            own = own + hop(row(chips + chip), -1, 0)
            own = own + hop(row(chips + (chip ^ far)), -1, far)
    return (
        found[1].reshape(tiles * cells),
        jnp.log(float(tiles) / own).reshape(cells),
    )


def solution(mesh):
    placed = (
        P(BOTH, None),
        P(BOTH, None),
        P(BOTH, None),
        P(BOTH, None),
        P(BOTH),
    )
    return jax.shard_map(
        step,
        mesh=mesh,
        in_specs=placed,
        out_specs=(P(BOTH), P(BOTH)),
        check_vma=False,
    )
```

```python
import functools
import math

import jax
import jax.numpy as jnp
from jax import lax
from jax.experimental import pallas as pl
from jax.experimental.pallas import tpu as pltpu
from jax.sharding import PartitionSpec as P


ITERS = 2
REGULARIZER = 0.05
EPSILON = 1e-06
CORES = 2
LANES = 128
MIB = 2**20
GROUP = 4
FIELD = 256
STRAIGHT = {3: 8}


BOTH = ("group", "member")
VM = pl.BlockSpec(memory_space=pltpu.VMEM)
SM = pl.BlockSpec(memory_space=pltpu.SMEM)
F32 = jnp.float32
BF16 = jnp.bfloat16
FACTOR = math.log2(math.e) / REGULARIZER


def odd(bits):
    return bin(bits).count("1") % 2


def odd_traced(value, size):
    result = value
    for b in range(1, size.bit_length()):
        result = result ^ (value >> b)
    return result & 1


def coded(pair_source, pair_target, pair_count, members, even):
    chip = lax.axis_index("member") // CORES
    beyond = (pair_target >= members).astype(jnp.int32)
    place = pair_target - beyond * members
    kind = odd_traced(place, members) ^ (beyond & even)
    late = beyond * (place // CORES != chip).astype(jnp.int32)
    slots = pair_source.shape[1]
    listed = (jnp.arange(slots, dtype=jnp.int32)[None] < pair_count[:, None]).astype(jnp.int32)
    entry = pair_source + (pair_target // CORES) * FIELD
    code = kind + 2 * late + 4 * listed + 8 * entry
    return jnp.concatenate([code, pair_count[:, None]], 1)


def entry_of(code):
    return code & (FIELD - 1), code // FIELD


def up_to_group(count):
    return -(-count // GROUP) * GROUP


def hop(x, up, bits):
    groups, members = lax.axis_size("group"), lax.axis_size("member")
    turn = odd(bits) ^ ((up & 1) if groups % 2 == 0 else 0)
    mask = CORES * bits + turn
    return lax.ppermute(
        x,
        BOTH,
        [
            (g * members + m, (g - up) % groups * members + (m ^ mask))
            for g in range(groups)
            for m in range(members)
        ],
    )


def pair_groups(x, odd_first):
    groups, members = lax.axis_size("group"), lax.axis_size("member")
    pairs = []
    for g in range(groups):
        other = (g + (1 if (g % 2 == 1) == odd_first else -1)) % groups
        pairs += [(g * members + m, other * members + (m ^ 1)) for m in range(members)]
    return lax.ppermute(x, BOTH, pairs)


def partner(x):
    size = lax.axis_size("member")
    return lax.ppermute(x, "member", [(i, i ^ 1) for i in range(size)])


def plan_of(chips):
    return {k: STRAIGHT.get(k, 0) for k in range(1, chips)}


def gathered(target, beyond, chips):
    own = []
    for k in range(1, chips):
        own.append(hop(target, 0, k))
    blocks = {}
    for k, eighths in plan_of(chips).items():
        cut = target.shape[0] * eighths // 8
        blocks[k] = []
        if cut > 0:
            blocks[k].append(hop(target[:cut], 1, k))
        if cut < target.shape[0]:
            blocks[k].append(hop(beyond[cut:], 0, k))
    return own, [blocks[k] for k in range(1, chips)]


def place(window, at, blocks):
    row = 0
    for block in blocks:
        rows = block.shape[0]
        window[at, row : row + rows] = unit(block[...])
        row += rows


def unit(values):
    floats = values.astype(F32)
    length = jnp.sqrt(jnp.sum(floats * floats, axis=1, keepdims=True) + EPSILON)
    return (floats * (1.0 / length)).astype(BF16)


def rows_out(acc, out):
    for s in range(out.shape[0]):
        out[s : s + 1] = jnp.sum(jnp.transpose(acc[s]), axis=0, keepdims=True)


def add_halves(acc, s, values):
    total = values[:, :LANES]
    for j in range(1, values.shape[1] // LANES):
        total = total + values[:, j * LANES : (j + 1) * LANES]
    acc[s] += total


def prepare_kernel(own, target, other, mine, theirs, units, home, first, second):
    cells = units.shape[1]
    tiles = own.shape[0] // cells
    slots = mine.shape[1] - 1
    kind = odd_traced(lax.axis_index("member"), lax.axis_size("member"))
    counts = (jnp.int32(0), jnp.int32(0))
    for half, info in enumerate((mine, theirs)):

        def step(m, counts, half=half, info=info):
            early, late = counts
            for i in range(math.gcd(slots, GROUP)):
                code = info[0, m * math.gcd(slots, GROUP) + i]
                hit = ((code & 5) == (4 | kind)).astype(jnp.int32)
                is_late = (code >> 1) & 1
                entry = (code >> 3) + half * tiles
                first[1 + early] = entry
                second[1 + late] = entry
                late_hit = hit & is_late
                early, late = early + hit - late_hit, late + late_hit
            return early, late

        group = math.gcd(slots, GROUP)
        counts = lax.fori_loop(0, (info[0, slots] + group - 1) // group, step, counts)
    first[0], second[0] = counts
    for s in range(tiles):
        units[s] = unit(own[s * cells : (s + 1) * cells])
        units[tiles + s] = unit(other[s * cells : (s + 1) * cells])
    home[...] = unit(target[...])


def build_pairs(units, window, table, factors, acc, where):
    spare = acc.shape[0] - 1
    found = table[0]

    def step(m, carry):
        for i in range(GROUP):
            n = m * GROUP + i
            real = n < found
            at = jnp.where(real, n, 0)
            s, w = entry_of(table[1 + at])
            logits = lax.dot_general(
                units[s], window[where(w)], (((1,), (1,)), ((), ())), preferred_element_type=F32
            )
            values = jnp.exp2(logits * FACTOR)
            factors[n] = values.astype(BF16)
            add_halves(acc, jnp.where(real, s, spare), values)
        return carry

    lax.fori_loop(0, (found + GROUP - 1) // GROUP, step, 0)


def first_kernel(chips, units, table, home, *refs):
    tiles = refs[:chips]
    factors, acc, window = refs[chips:]
    chip = lax.axis_index("member") // CORES
    window[chip] = home[...]
    for k in range(1, chips):
        window[chip ^ k] = unit(tiles[k - 1][...])
    window[chips] = unit(tiles[chips - 1][...])
    acc[...] = jnp.zeros_like(acc)
    build_pairs(units, window, table, factors, acc, lambda w: jnp.minimum(w, chips))


def second_kernel(shape, units, table, before, *refs):
    chips = len(shape) + 1
    tiles = list(refs[: sum(shape)])
    factors, rows, acc, window = refs[sum(shape) :]
    chip = lax.axis_index("member") // CORES
    for k, count in enumerate(shape):
        place(window, chip ^ (k + 1), [tiles.pop(0) for _ in range(count)])
    acc[...] = before[...]
    build_pairs(units, window, table, factors, acc, lambda w: w - chips)
    rows_out(acc, rows)


def row_kernel(
    paired, first, second, lists_first, lists_second, columns, wide, near, rows, scale, acc
):
    chips = columns.shape[0] // 2
    tiles = acc.shape[0] // CORES
    below, above = wide[...], near[...]
    if paired:
        swapped = (lax.axis_index("group") & 1) == 1
        below, above = jnp.where(swapped, above, below), jnp.where(swapped, below, above)
    scale[:chips] = float(tiles) / (columns[:chips] + below[chips:])
    scale[chips:] = float(tiles) / (columns[chips:] + above[:chips])
    acc[...] = jnp.zeros_like(acc)
    for factors, table in ((first, lists_first), (second, lists_second)):

        def pair(n, carry, factors=factors, table=table):
            s, w = entry_of(table[1 + n])
            add_halves(acc, s, factors[n].astype(F32) * scale[pl.ds(w, 1), :])
            return carry

        lax.fori_loop(0, table[0], pair, 0)
    rows_out(acc, rows)


def column_kernel(last, first, second, lists_first, lists_second, rows, arrived, columns, *rest):
    if last:
        logs, spread, acc = rest
    else:
        spread, acc = rest
    tiles = rows.shape[0] // CORES
    cells = first.shape[1]
    total = rows[...] + jnp.concatenate([arrived[tiles:], arrived[:tiles]], 0)
    scale = 1.0 / total
    if last:
        logs[...] = jnp.log(scale[:tiles] * float(cells))
    for s in range(CORES * tiles):
        spread[s] = jnp.transpose(jnp.broadcast_to(scale[s : s + 1], (LANES, cells)))
    acc[...] = jnp.zeros_like(acc)
    spare = acc.shape[0] - 1
    for factors, table in ((first, lists_first), (second, lists_second)):
        found = table[0]

        def step(m, carry, factors=factors, table=table, found=found):
            for i in range(GROUP):
                n = m * GROUP + i
                real = n < found
                s, w = entry_of(table[1 + jnp.where(real, n, 0)])
                w = jnp.where(real, w, spare)
                values = factors[n].astype(F32)
                for j in range(cells // LANES):
                    part = values[:, j * LANES : (j + 1) * LANES] * spread[s]
                    acc[w, :, j * LANES : (j + 1) * LANES] += jnp.sum(
                        part.reshape(cells // 8, 8, LANES), axis=0
                    )
            return carry

        lax.fori_loop(0, (found + GROUP - 1) // GROUP, step, 0)
    columns[...] = jnp.sum(acc[:spare], axis=1)


def step(source, target, pair_source, pair_target, pair_count):
    groups, members = lax.axis_size("group"), lax.axis_size("member")
    chips = members // CORES
    cells, width = target.shape
    tiles = source.shape[0] // cells
    both = CORES * tiles
    slots = pair_source.shape[1]
    even = 1 if groups % 2 == 0 else 0
    most_first = up_to_group(min(CORES * slots, both * (chips + 1)))
    most_second = up_to_group(min(CORES * slots, both * (chips - 1)))

    beyond = hop(target, 1, 0)
    own_tiles, next_tiles = gathered(target, beyond, chips)
    info = coded(pair_source, pair_target, pair_count, members, even)
    partner_source = partner(source)
    stay = [(i, i) for i in range(members)]
    own_source = lax.ppermute(source, "member", stay)
    own_target = lax.ppermute(target, "member", stay)
    partner_info = partner(info)

    def shaped(*dims, kind=F32):
        return jax.ShapeDtypeStruct(dims, kind)

    def limit(size):
        return pltpu.CompilerParams(vmem_limit_bytes=int(size))

    def cost(pairs):
        return pl.CostEstimate(
            flops=2 * pairs * cells * cells * width,
            transcendentals=pairs * cells * cells,
            bytes_accessed=pairs * cells * cells * 2,
        )

    tile = cells * width * 2
    lanes_acc = (both, cells, LANES)
    prepare = pl.pallas_call(
        prepare_kernel,
        out_shape=(
            shaped(both, cells, width, kind=BF16),
            shaped(cells, width, kind=BF16),
            shaped(2 + most_first, kind=jnp.int32),
            shaped(2 + most_second, kind=jnp.int32),
        ),
        in_specs=[VM, VM, VM, SM, SM],
        out_specs=(VM, VM, SM, SM),
        compiler_params=limit(4 * MIB),
        cost_estimate=cost(both),
        name="prepare",
    )
    units, home, lists_first, lists_second = prepare(
        own_source, own_target, partner_source, info, partner_info
    )

    early = own_tiles + [beyond]
    late = [block for blocks in next_tiles for block in blocks]
    first_call = pl.pallas_call(
        functools.partial(first_kernel, chips),
        out_shape=(shaped(most_first, cells, cells, kind=BF16), shaped(both + 1, cells, LANES)),
        in_specs=[VM, SM, VM] + [VM] * len(early),
        out_specs=(VM, VM),
        scratch_shapes=[pltpu.VMEM((chips + 1, cells, width), BF16)],
        compiler_params=limit((most_first + 2 * chips + 2 + both) * tile + 5 * MIB),
        cost_estimate=cost(most_first),
        name="first",
    )
    first, acc = first_call(units, lists_first, home, *early)
    second, rows = pl.pallas_call(
        functools.partial(second_kernel, [len(blocks) for blocks in next_tiles]),
        out_shape=(shaped(most_second, cells, cells, kind=BF16), shaped(both, cells)),
        in_specs=[VM, SM, VM] + [VM] * len(late),
        out_specs=(VM, VM),
        scratch_shapes=[
            pltpu.VMEM((both + 1, cells, LANES), F32),
            pltpu.VMEM((chips, cells, width), BF16),
        ],
        compiler_params=limit((most_second + 2 * chips + both) * tile + 5 * MIB),
        cost_estimate=cost(most_second),
        name="second",
    )(units, lists_second, acc, *late)
    held = (first, second, lists_first, lists_second)
    held_limit = limit((most_first + most_second) * tile + 4 * MIB)

    for sweep in range(ITERS):
        last = sweep + 1 == ITERS
        if sweep > 0:
            rows = pl.pallas_call(
                functools.partial(row_kernel, even == 1),
                out_shape=shaped(both, cells),
                in_specs=[VM, VM, SM, SM, VM, VM, VM],
                out_specs=VM,
                scratch_shapes=[pltpu.VMEM((2 * chips, cells), F32), pltpu.VMEM(lanes_acc, F32)],
                compiler_params=held_limit,
                name="rows",
            )(*held, columns, wide, near)
        found = pl.pallas_call(
            functools.partial(column_kernel, last),
            out_shape=(shaped(2 * chips, cells),) + ((shaped(tiles, cells),) if last else ()),
            in_specs=[VM, VM, SM, SM, VM, VM],
            out_specs=(VM,) + ((VM,) if last else ()),
            scratch_shapes=[
                pltpu.VMEM(lanes_acc, F32),
                pltpu.VMEM((2 * chips + 1, 8, cells), F32),
            ],
            compiler_params=held_limit,
            name="columns",
        )(*held, rows, partner(rows))
        columns = found[0]
        bits = [1 << b for b in range(chips.bit_length() - 1)]
        if not last:
            if chips == 4:
                shares = []
                for k in (3, 1, 2):
                    shares.append(hop(columns, 0, k))
                columns = columns + shares[0] + shares[1] + shares[2]
            else:
                for bit in bits:
                    columns = columns + hop(columns, 0, bit)
            wide = pair_groups(columns, True) if even else hop(columns, -1, 0)
            near = pair_groups(columns, False) if even else hop(columns, 1, 0)
        else:
            chip = lax.axis_index("member") // CORES
            for bit in bits[1:]:
                columns = columns + hop(columns, 0, bit)
            far = bits[0]

            def row(index):
                return lax.dynamic_slice_in_dim(columns, index, 1, 0)

            own = row(chip)
            own = own + hop(row(chip ^ far), 0, far)
            own = own + hop(row(chips + chip), -1, 0)
            own = own + hop(row(chips + (chip ^ far)), -1, far)
    return (
        found[1].reshape(tiles * cells),
        jnp.log(float(tiles) / own).reshape(cells),
    )


def solution(mesh):
    placed = (
        P(BOTH, None),
        P(BOTH, None),
        P(BOTH, None),
        P(BOTH, None),
        P(BOTH),
    )
    return jax.shard_map(
        step,
        mesh=mesh,
        in_specs=placed,
        out_specs=(P(BOTH), P(BOTH)),
        check_vma=False,
    )
```
